32 devices in a mesh: seq: 4 (over z), head: 2 (over core), dp: 4 (over y, x).
Axes of the slice: x: 2, y: 2, z: 4, core: 2. Of those that a mesh axis runs over, the one named last changes fastest.
Arguments:
- hidden: bfloat16 [4, 768, 1024], P('dp', 'seq'), may hold values from -6 to 6
- norm_gain: float32 [1024], replicated, may hold values from 0.5 to 1.5
- projection: bfloat16 [3, 1024, 1024], P(None, None, 'head'), may hold values from -1 to 1
- upstream: bfloat16 [4, 768, 1024], P('dp', 'seq', 'head'), may hold values from -6 to 6
- cluster: int32 [4, 768, 1], P('dp', 'seq'), may hold values from 0 to 3; in each aligned block of 192 rows (0 to 191, 192 to 383, ..., all dimensions but the last counted through in order) at most 144 rows name the same one
Outputs:
- input_gradient: bfloat16 [4, 768, 1024], P('dp', 'seq', 'head')
- gain_gradient: float32 [1024], P('head')
The draws below stay inside these ranges and needn't reach their ends.
Inputs may be any that keep to these rules, and one draw needn't show every extreme that they name: Among the 192 tokens of one device no cluster is named more than 144 times, a bound that some block reaches.
All inputs are finite; a program needn't handle non-finite values.
Results may differ from the reference program's by a relative error of at most 0.01.
The reference program's roundings to bfloat16 on the way count: a program that leaves them out, or rounds other values in their place, can miss the bound.
Values may be sent and summed in bfloat16 or wider, within the bound.
A program may use at most 64 MiB of HBM per device.

```python
import math
import jax
import jax.numpy as jnp
import numpy as np
from jax import lax

D = 1024
HDIM = 64
TOK_DEV = 192
CLUSTERS = 4
HE = 1024
GROUP_HEADS = 8
LEN = 768
SEQS = 4
SLOT = 144
ROWS = 576
N_HEAD = 2


def draw_hidden(key, part):
    samples = jax.random.normal(jax.random.fold_in(key, 1), (SEQS, LEN, D), jnp.float32)
    return jnp.clip(samples, -6.0, 6.0).astype(jnp.bfloat16)


def draw_projection(key, part):
    weights_base = jax.random.normal(jax.random.fold_in(key, 11), (3, D, HE), jnp.float32) / math.sqrt(D)
    return jnp.clip(weights_base, -1.0, 1.0).astype(jnp.bfloat16)


def levels(stream_key, shape, shards, low, top_value):
    def one(axis_at, blocks):
        steps = jax.random.uniform(jax.random.fold_in(jax.random.fold_in(stream_key, 6), axis_at), (blocks,), jnp.float32, low / len(shards), top_value / len(shards))
        return jnp.repeat(jnp.exp(steps), shape[axis_at] // blocks).reshape((-1,) + (1,) * (len(shape) - axis_at - 1))

    loudness = one(*shards[0])
    for cut in shards[1:]:
        loudness = loudness * one(*cut)
    return loudness


def deal_out(stream_key, own, number, rows, count, top, reach, skew):
    ranking = jax.random.permutation(stream_key, count)
    heavy_load, ordinary = portions_of(count, rows * top, reach, skew, True), portions_of(count, rows * top, reach, skew, False)
    places = jnp.arange(count)

    def named(lengths, offset_by):
        used = int((lengths > 0).sum())
        fixed = max(1, used // 4)
        passed = fixed + (places - fixed + offset_by * (used - fixed)) % max(1, count - fixed)
        return jnp.zeros((count,), jnp.int32).at[ranking[jnp.where(places < fixed, places, passed)]].set(jnp.asarray(lengths, jnp.int32))

    lengths = jnp.where(number % 4 == 0, named(heavy_load, number // 4), named(ordinary, number - number // 4 - 1))
    mixed = jax.random.permutation(jax.random.fold_in(own, 3), count)
    source_of, taker = mixed[0:count // 2 * 2:2], mixed[1:count // 2 * 2:2]
    room = jnp.minimum(lengths[source_of] - 1, reach - lengths[taker]) // 2
    room = jnp.where((source_of == ranking[0]) | (taker == ranking[0]) | (lengths[taker] == 0), 0, jnp.maximum(room, 0))
    passed = jax.random.randint(jax.random.fold_in(own, 4), (count // 2,), 0, 1 << 20) % (room + 1)
    lengths = lengths.at[source_of].add(-passed).at[taker].add(passed)
    items = jnp.searchsorted(jnp.cumsum(lengths), jnp.arange(rows * top), side="right").astype(jnp.int32)
    listing = items.reshape(top, rows).T
    listing = listing[jax.random.permutation(jax.random.fold_in(own, 1), rows)]
    offset_by = jax.random.randint(jax.random.fold_in(own, 2), (rows, 1), 0, top)
    return jnp.take_along_axis(listing, (jnp.arange(top)[None, :] + offset_by) % top, axis=1)


def portions_of(number_of, total, bound, skew, full):
    loads = [(1 << 20) // math.isqrt(grade ** skew) + 1 for grade in range(1, number_of + 1)]
    largest = bound if full else min(bound, max(-(-total // number_of), total * loads[0] // sum(loads)))
    least = 1 if total - largest >= number_of - 1 else 0
    given, spare = [largest] + [least] * (number_of - 1), total - largest - least * (number_of - 1)
    while spare > 0:
        free = [i for i in range(1, number_of) if given[i] < largest] or [i for i in range(1, number_of) if given[i] < bound]
        whole, left = sum([loads[i] for i in free]), spare
        for i in free:
            extra = min(bound - given[i], max(1, left * loads[i] // whole), spare)
            given[i] = given[i] + extra
            spare = spare - extra
    return np.array(given)


def gaussian(own_key, shape, deviation, most, split=(), held_as=jnp.bfloat16):
    drawn = deviation * jax.random.normal(own_key, shape, jnp.float32)
    if split:
        drawn = drawn * levels(own_key, shape, split, -0.22, 0.18)
    return jnp.clip(drawn, -most, most).astype(held_as)


def setup_inputs(seed: int = 0) -> dict:
    splits = jax.random.split(jax.random.key(seed), 6)
    hidden = draw_hidden(jax.random.fold_in(splits[5], 71), 0)
    norm_gain = jnp.clip(1.0 + 0.1 * jax.random.normal(splits[1], (D,), jnp.float32), 0.5, 1.5)
    projection = draw_projection(jax.random.fold_in(splits[5], 71), 0)
    upstream = gaussian(splits[3], (SEQS, LEN, HE), 1.0, 6.0, ((0, 4), (1, 4), (2, 2)))
    cluster_keys = jax.random.split(jax.random.fold_in(splits[4], 1), SEQS * LEN // TOK_DEV)
    cluster_turns = jax.random.permutation(jax.random.fold_in(splits[4], 3), SEQS * LEN // TOK_DEV)
    cluster = jax.vmap(lambda own, number: deal_out(jax.random.fold_in(splits[4], 2), own, number, TOK_DEV, CLUSTERS, 1, SLOT, 2))(cluster_keys, cluster_turns).reshape((SEQS, LEN, 1))
    return dict(hidden=hidden, norm_gain=norm_gain, projection=projection, upstream=upstream, cluster=cluster)


epsilon = 1e-05
masked = -1e+30

def normalize(values, norm_gain):
    values = values.astype(jnp.float32)
    center = values - lax.optimization_barrier(jnp.mean(values, -1, keepdims=True))
    spread = lax.rsqrt(lax.optimization_barrier(jnp.mean(center * center, -1, keepdims=True)) + epsilon)
    scaled = center * spread
    return (scaled, spread, (scaled * norm_gain).astype(jnp.bfloat16))

def attend_backward(queries, key_rows, values, upstream, allowed, factor):
    scores = lax.dot_general(queries, key_rows, (((1,), (1,)), ((), ())), preferred_element_type=jnp.float32) * factor
    scores = jnp.where(allowed, scores, masked)
    powers = jnp.exp(scores - lax.optimization_barrier(jnp.max(scores, -1, keepdims=True)))
    weights = powers / lax.optimization_barrier(jnp.sum(powers, -1, keepdims=True))
    rounded = weights.astype(jnp.bfloat16)
    output = jnp.dot(rounded, values, preferred_element_type=jnp.float32)
    center_term = lax.optimization_barrier(jnp.sum(upstream.astype(jnp.float32) * output, -1, keepdims=True))
    grad_values = lax.dot_general(rounded, upstream, (((0,), (0,)), ((), ())), preferred_element_type=jnp.float32).astype(jnp.bfloat16)
    grad_weights = lax.dot_general(upstream, values, (((1,), (1,)), ((), ())), preferred_element_type=jnp.float32)
    grad_scores = (weights * (grad_weights - center_term) * factor).astype(jnp.bfloat16)
    grad_queries = jnp.dot(grad_scores, key_rows, preferred_element_type=jnp.float32).astype(jnp.bfloat16)
    grad_keys = lax.dot_general(grad_scores, queries, (((0,), (0,)), ((), ())), preferred_element_type=jnp.float32).astype(jnp.bfloat16)
    return (grad_queries, grad_keys, grad_values)

def cluster_grads(payload, validity, head_width):
    row_count = payload.shape[0]
    spans = payload.shape[1] // 4
    heads_local = spans // head_width
    positions = lax.broadcasted_iota(jnp.int32, (row_count, row_count), 0)
    others = lax.broadcasted_iota(jnp.int32, (row_count, row_count), 1)
    allowed = (positions >= others) & (validity[None, :] > 0)
    factor = head_width ** (-0.5)

    def one_head(head_index, result):
        offset = head_index * head_width

        def select(portion):
            return lax.dynamic_slice_in_dim(payload, portion * spans + offset, head_width, 1)
        grads_head = attend_backward(select(0), select(1), select(2), select(3), allowed, factor)
        for portion in range(3):
            result = lax.dynamic_update_slice_in_dim(result, grads_head[portion], portion * spans + offset, 1)
        return result
    return lax.fori_loop(0, heads_local, one_head, jnp.zeros((row_count, 3 * spans), jnp.bfloat16))

def reference(hidden, norm_gain, projection, upstream, cluster):
    scaled, spread, normed = normalize(hidden, norm_gain)
    flattened = normed.reshape(-1, D)
    projected = [jnp.dot(flattened, projection[portion], preferred_element_type=jnp.float32).astype(jnp.bfloat16).reshape(SEQS, LEN, HE) for portion in range(3)]
    group_width = GROUP_HEADS * HDIM
    gradients = []
    for sequence in range(SEQS):
        labels = cluster[sequence, :, 0]
        member = (labels[:, None] == jnp.arange(CLUSTERS, dtype=jnp.int32)[None, :]).astype(jnp.int32)
        counts = lax.optimization_barrier(jnp.sum(member, 0)).astype(jnp.int32)
        ordering = jnp.argsort(labels, stable=True).astype(jnp.int32)
        starts = (jnp.cumsum(counts) - counts).astype(jnp.int32)
        within = jnp.arange(ROWS, dtype=jnp.int32)
        validity = within[None, :] < counts[:, None]
        source_rows = jnp.where(validity, ordering[jnp.minimum(starts[:, None] + within[None, :], LEN - 1)], LEN).astype(jnp.int32)
        payload = jnp.concatenate([projected[0][sequence], projected[1][sequence], projected[2][sequence], upstream[sequence]], 1)
        padded = jnp.concatenate([payload, jnp.zeros((1, 4 * HE), jnp.bfloat16)], 0)

        def per_cluster(entries):
            return cluster_grads(padded[entries[0]], entries[1].astype(jnp.float32), HDIM)
        cluster_out = lax.map(per_cluster, (source_rows, validity))
        restored = jnp.zeros((LEN + 1, 3 * HE), jnp.bfloat16).at[source_rows.reshape(-1)].set(cluster_out.reshape(-1, 3 * HE))[:LEN]
        partial_value = jnp.zeros((LEN, D), jnp.float32)
        for group_index in range(N_HEAD):
            column_start = group_index * group_width
            group_term = jnp.zeros((LEN, D), jnp.float32)
            for portion in range(3):
                first = portion * HE + column_start
                group_term = group_term + jnp.dot(restored[:, first:first + group_width], projection[portion][:, column_start:column_start + group_width].T, preferred_element_type=jnp.float32)
            partial_value = partial_value + lax.optimization_barrier(group_term.astype(jnp.bfloat16)).astype(jnp.float32)
        gradients.append(partial_value)
    grad_normed = jnp.stack(gradients, 0)
    gain_gradient = lax.optimization_barrier(jnp.sum(grad_normed * scaled, (0, 1))) * (SEQS * LEN) ** (-0.5)
    grad_scaled = grad_normed * norm_gain
    first_mean = lax.optimization_barrier(jnp.mean(grad_scaled, -1, keepdims=True))
    second_mean = lax.optimization_barrier(jnp.mean(grad_scaled * scaled, -1, keepdims=True))
    input_gradient = (spread * (grad_scaled - first_mean - scaled * second_mean)).astype(jnp.bfloat16)
    return (input_gradient, gain_gradient)
```

```python
import functools

import jax
import jax.numpy as jnp
from jax import lax
from jax.experimental import pallas as pl
from jax.experimental.pallas import tpu as pltpu
from jax.sharding import PartitionSpec as P

HDIM = 64
CLUS_DEV = 1


epsilon = 1e-05
masked = -1e30


def normalize(values, norm_gain):
    values = values.astype(jnp.float32)
    center = values - jnp.mean(values, -1, keepdims=True)
    spread = lax.rsqrt(jnp.mean(center * center, -1, keepdims=True) + epsilon)
    scaled = center * spread
    return (scaled, spread, (scaled * norm_gain).astype(jnp.bfloat16))


def attend_backward(queries, key_rows, values, upstream, allowed, factor):
    scores = (
        lax.dot_general(
            queries, key_rows, (((1,), (1,)), ((), ())), preferred_element_type=jnp.float32
        )
        * factor
    )
    scores = jnp.where(allowed, scores, masked)
    powers = jnp.exp(scores - jnp.max(scores, -1, keepdims=True))
    weights = powers / jnp.sum(powers, -1, keepdims=True)
    rounded = weights.astype(jnp.bfloat16)
    output = jnp.dot(rounded, values, preferred_element_type=jnp.float32)
    center_term = jnp.sum(upstream.astype(jnp.float32) * output, -1, keepdims=True)
    grad_values = lax.dot_general(
        rounded, upstream, (((0,), (0,)), ((), ())), preferred_element_type=jnp.float32
    ).astype(jnp.bfloat16)
    grad_weights = lax.dot_general(
        upstream, values, (((1,), (1,)), ((), ())), preferred_element_type=jnp.float32
    )
    grad_scores = (weights * (grad_weights - center_term) * factor).astype(jnp.bfloat16)
    grad_queries = jnp.dot(grad_scores, key_rows, preferred_element_type=jnp.float32).astype(
        jnp.bfloat16
    )
    grad_keys = lax.dot_general(
        grad_scores, queries, (((0,), (0,)), ((), ())), preferred_element_type=jnp.float32
    ).astype(jnp.bfloat16)
    return (grad_queries, grad_keys, grad_values)


def cluster_grads(payload, validity, head_width):
    row_count = payload.shape[0]
    spans = payload.shape[1] // 4
    heads_local = spans // head_width
    positions = lax.broadcasted_iota(jnp.int32, (row_count, row_count), 0)
    others = lax.broadcasted_iota(jnp.int32, (row_count, row_count), 1)
    allowed = (positions >= others) & (validity[None, :] > 0)
    factor = head_width ** (-0.5)

    def one_head(head_index, result):
        offset = head_index * head_width

        def select(portion):
            return lax.dynamic_slice_in_dim(payload, portion * spans + offset, head_width, 1)

        grads_head = attend_backward(select(0), select(1), select(2), select(3), allowed, factor)
        for portion in range(3):
            result = lax.dynamic_update_slice_in_dim(
                result, grads_head[portion], portion * spans + offset, 1
            )
        return result

    return lax.fori_loop(0, heads_local, one_head, jnp.zeros((row_count, 3 * spans), jnp.bfloat16))


def on_device(hidden, norm_gain, projection, upstream, cluster):
    seq_count = lax.axis_size("seq")
    tokens = hidden.shape[1]
    width_model = hidden.shape[2]
    spans = projection.shape[2]
    clusters_all = CLUS_DEV * seq_count
    slot_rows = 3 * tokens // clusters_all
    scaled, spread, normed = normalize(hidden[0], norm_gain)
    labels = cluster[0, :, 0]
    member = (labels[:, None] == jnp.arange(clusters_all, dtype=jnp.int32)[None, :]).astype(
        jnp.int32
    )
    ranks = jnp.sum(jnp.cumsum(member, 0) * member, 1) - 1
    target = labels * slot_rows + ranks
    projected = jnp.einsum(
        "td,kdh->tkh", normed, projection, preferred_element_type=jnp.float32
    ).astype(jnp.bfloat16)
    payload = jnp.concatenate([projected.reshape(tokens, 3 * spans), upstream[0]], 1)
    columns = payload.shape[1]
    outgoing = jnp.zeros((clusters_all * slot_rows, columns), jnp.bfloat16).at[target].set(payload)
    outgoing = outgoing.reshape(seq_count, CLUS_DEV, slot_rows, columns)
    present = jnp.zeros((clusters_all * slot_rows,), jnp.bfloat16).at[target].set(1.0)
    present = present.reshape(seq_count, CLUS_DEV, slot_rows)
    rows_in = lax.all_to_all(outgoing, "seq", split_axis=0, concat_axis=0, tiled=True)
    marks_in = lax.all_to_all(present, "seq", split_axis=0, concat_axis=0, tiled=True)
    sources = rows_in.shape[0]
    item_count = rows_in.shape[1]
    stacked = jnp.swapaxes(rows_in, 0, 1).reshape(item_count, sources * slot_rows, rows_in.shape[3])
    mark_rows = jnp.swapaxes(marks_in, 0, 1).reshape(item_count, sources * slot_rows)

    def per_item(entries):
        return cluster_grads(entries[0], entries[1].astype(jnp.float32), HDIM)

    results = lax.map(per_item, (stacked, mark_rows))
    results = jnp.einsum(
        "irkh,kdh->ird",
        results.reshape(item_count, sources * slot_rows, 3, spans),
        projection,
        preferred_element_type=jnp.float32,
    ).astype(jnp.bfloat16)
    width_out = results.shape[-1]
    results = results.reshape(item_count, sources, slot_rows, width_out)
    answer = jnp.swapaxes(results, 0, 1)
    returned = lax.all_to_all(answer, "seq", split_axis=0, concat_axis=0, tiled=True)
    restored = returned.reshape(clusters_all * slot_rows, width_model)[target]
    partial_value = restored.astype(jnp.float32)
    half_width = width_model // lax.axis_size("head")
    offset = lax.axis_index("head") * half_width
    own_scaled = lax.dynamic_slice_in_dim(scaled, offset, half_width, 1)
    own_gain = lax.dynamic_slice_in_dim(norm_gain, offset, half_width, 0)
    gradient = lax.psum_scatter(
        partial_value.astype(jnp.bfloat16), "head", scatter_dimension=1, tiled=True
    ).astype(jnp.float32)
    scaled_grad = gradient * own_gain
    first_sum, second_sum = lax.psum(
        (
            jnp.sum(scaled_grad, -1, keepdims=True),
            jnp.sum(scaled_grad * own_scaled, -1, keepdims=True),
        ),
        "head",
    )
    first_mean = first_sum / width_model
    second_mean = second_sum / width_model
    input_gradient = (spread * (scaled_grad - first_mean - own_scaled * second_mean)).astype(
        jnp.bfloat16
    )
    local_sum = jnp.sum(gradient * own_scaled, 0)
    gain_total = lax.psum(local_sum, ("seq", "dp"))
    gain_gradient = gain_total * (seq_count * lax.axis_size("dp") * tokens) ** (-0.5)
    return (input_gradient.reshape(1, tokens, half_width), gain_gradient)


MESH = pl.DeviceIdType.MESH
LANES = 128
RECEIVED = 16
COLUMNS = 256
QU, KE, VA = range(3)
NT = (((1,), (1,)), ((), ()))
TN = (((0,), (0,)), ((), ()))


def dot(left, right, dims=(((1,), (0,)), ((), ()))):
    return lax.dot_general(left, right, dims, preferred_element_type=jnp.float32)


def fused(
    n_seq, n_head, n_dp, total_rows,
    hidden_hbm, gain_hbm, proj_hbm, up_hbm, cluster_hbm,
    grad_ref, gain_out_ref,
    hidden_ref, gain_ref, cluster_ref, w_ref, scaled_ref, up_ref, own, keys_in, rows_in,
    labels_out, labels_in, bias, powers_ref, small, stats_in, final_in,
    dq_out, dq_in, dkv_out, dkv_in, acc, gback,
    part_acc, part_out, part_in, spread_ref, gain_src, gain_seq, gain_mid, gain_all, gain_sum,
    in_sem, w_sem, t_send, t_recv, l_sem, h_send, h_recv, s_sem, d_sem,
):
    me = lax.axis_index("seq")
    core = lax.axis_index("head")
    group = lax.axis_index("dp")
    tokens, width = hidden_hbm.shape
    pairs = up_hbm.shape[1] // LANES
    half = width // n_head
    factor = HDIM ** (-0.5)
    middle_pair = pairs // 2
    low, high = range(middle_pair), range(middle_pair, pairs)

    barrier = pltpu.get_barrier_semaphore()
    along = [{"seq": lax.rem(me + o, n_seq)} for o in range(1, n_seq)]
    across = [
        {"dp": lax.rem(group + o // n_head, n_dp), "head": lax.rem(core + o % n_head, n_head)}
        for o in range(1, n_dp * n_head)
    ]
    for peer in along + across:
        pl.semaphore_signal(barrier, inc=1, device_id=peer, device_id_type=MESH)

    upper = lax.div(me, n_seq // 2)
    load_up = pltpu.make_async_copy(up_hbm, up_ref, in_sem.at[0])
    load_hidden = pltpu.make_async_copy(hidden_hbm, hidden_ref, in_sem.at[1])
    load_gain = pltpu.make_async_copy(gain_hbm, gain_ref, in_sem.at[2])
    load_cluster = pltpu.make_async_copy(cluster_hbm, cluster_ref, in_sem.at[3])
    order = [lax.rem(1 - upper + i, 3) for i in range(3)]
    w_copies = [pltpu.make_async_copy(proj_hbm.at[p], w_ref.at[p], w_sem.at[p]) for p in order]
    for copy in (load_up, load_hidden, load_gain, *w_copies, load_cluster):
        copy.start()

    def remote(src, dst, send, recv, peer):
        return pltpu.make_async_remote_copy(
            src_ref=src, dst_ref=dst, send_sem=send, recv_sem=recv,
            device_id=peer, device_id_type=MESH,
        )

    def lanes(pair):
        return slice(pair * LANES, (pair + 1) * LANES)

    def block(j):
        return slice(j * tokens, (j + 1) * tokens)

    def place(pair):
        return pair % middle_pair

    numbers = [{} for _ in range(n_seq)]
    started = [[0, 0, 0] for _ in range(n_seq)]

    def transfer(key, src, dst, target, group_at):
        at = numbers[target].setdefault(key, len(numbers[target]))
        return remote(
            src, dst, t_send.at[group_at], t_recv.at[at], {"seq": jnp.int32(target)}
        )

    def send(source, key, src, dst, target, group_at):
        started[source][group_at] += 1
        transfer((source, *key), src, dst, target, group_at).start()

    def wait(source, target, key, dst):
        transfer((source, *key), dst, dst, target, 0).wait_recv()

    def send_own(source, target, kind, pair, spot):
        dst = keys_in.at[kind - KE, place(pair), block(spot)]
        send(source, ("keys", pair), own.at[kind * pairs + pair], dst, target, 0)

    def wait_keys(source, target, pair, spot):
        wait(source, target, ("keys", pair), keys_in.at[:, place(pair), block(spot)])

    def send_rows(source, target, kind, pair, slot):
        src = up_ref.at[:, lanes(pair)] if kind == 1 else own.at[QU * pairs + pair]
        send(source, ("rows", pair), src, rows_in.at[kind, slot, place(pair)], target, 0)

    def wait_rows(source, target, pair, slot):
        wait(source, target, ("rows", pair), rows_in.at[:, slot, place(pair)])

    def dispatch(stage, chips):
        for chip in chips:
            pl.when(me == chip)(functools.partial(stage, chip))

    def send_early(chip):
        for pair, target, slot in ((0, 1, chip - 2), (2, 2, 0))[: chip - 1]:
            send_rows(chip, target, 1, pair, slot)

    def send_queries(chip):
        for pair, target, slot in ((0, 1, chip - 2), (2, 2, 0))[: chip - 1]:
            send_rows(chip, target, 0, pair, slot)

    load_up.wait()

    @pl.when(upper == 1)
    def _():
        pl.semaphore_wait(barrier, len(along) + len(across))

    dispatch(send_early, (2, 3))

    load_hidden.wait()
    load_gain.wait()
    values = hidden_ref[...].astype(jnp.float32)
    center = values - jnp.mean(values, -1, keepdims=True)
    spread = lax.rsqrt(jnp.mean(center * center, -1, keepdims=True) + epsilon)
    scaled = center * spread
    scaled_ref[...] = scaled
    spread_ref[...] = jnp.broadcast_to(spread, spread_ref.shape)
    normed = (scaled * gain_ref[...]).astype(jnp.bfloat16)
    for i, p in enumerate(order):
        w_copies[i].wait()
        made = dot(normed, w_ref[p]).astype(jnp.bfloat16)
        for j in range(pairs):
            own[p * pairs + j] = made[:, lanes(j)]
        if i == 0:
            dispatch(send_queries, (2, 3))
    load_cluster.wait()
    labels = cluster_ref[...].astype(jnp.float32)
    labels = jnp.concatenate([labels, labels], 1)
    labels_out[...] = jnp.zeros_like(labels_out)
    labels_out[:1, :] = labels
    small[...] = jnp.zeros_like(small)

    @pl.when(upper == 0)
    def _():
        pl.semaphore_wait(barrier, len(along) + len(across))

    lane_head = lax.broadcasted_iota(jnp.int32, (1, LANES), 1) // HDIM
    head_masks = [jnp.where(lane_head == h, 1.0, 0.0).astype(jnp.bfloat16) for h in range(2)]
    factor_masks = [mask * jnp.bfloat16(factor) for mask in head_masks]
    label_copies = [
        remote(labels_out, labels_in.at[me], l_sem.at[0], l_sem.at[1], peer) for peer in along
    ]

    def stacked(rows, masks):
        return jnp.concatenate([rows * mask for mask in masks], 0)

    def role(chip):
        def statistics(source, target, pair, slot):
            dst = stats_in.at[slot, place(pair)]
            if source == chip:
                send(chip, ("stats", pair), small.at[pair], dst, target, 2)
            else:
                wait(source, chip, ("stats", pair), dst)

        def finals(source, target, pair, slot):
            if source == chip:
                src = small.at[pairs + slot * middle_pair + place(pair)]
                send(chip, ("final", pair), src, final_in.at[pair], target, 2)
            else:
                wait(source, chip, ("final", pair), final_in.at[pair])

        def dq_part(source, target, pair, slot, value=None):
            if source == chip:
                dq_out[slot, place(pair)] = value.astype(jnp.bfloat16)
                send(chip, ("dq", pair), dq_out.at[slot, place(pair)], dq_in.at[pair], target, 1)
            else:
                wait(source, chip, ("dq", pair), dq_in.at[pair])

        def dkv_send(target, pair, spot, sums):
            for kind in (1, 0):
                dkv_out[kind, place(pair), spot] = sums[kind + 1][block(spot)].astype(jnp.bfloat16)
                src = dkv_out.at[kind, place(pair), spot]
                send(chip, ("dkv", pair), src, dkv_in.at[kind, pair], target, 1)

        def dkv_wait(source, pair):
            wait(source, chip, ("dkv", pair), dkv_in.at[:, pair])

        def one_hot(j):
            row = labels_out[:1, :] if j == chip else labels_in[j, :1, :]
            classes = lax.broadcasted_iota(jnp.int32, (16, 2 * tokens), 0).astype(jnp.float32)
            return jnp.where(classes == row, 1.0, 0.0).astype(jnp.bfloat16)

        def make_bias(slot, spot, j, row):
            allowed = dot(one_hot(j)[:, :tokens], one_hot(row), TN) > 0.5
            if j == row:
                key_at = lax.broadcasted_iota(jnp.int32, (tokens, 2 * tokens), 0)
                row_at = lax.broadcasted_iota(jnp.int32, (tokens, 2 * tokens), 1)
                row_at = jnp.where(row_at >= tokens, row_at - tokens, row_at)
                allowed = allowed & (key_at <= row_at)
            bias[slot, block(spot), :] = jnp.where(allowed, 0.0, masked)

        def products(keys, query, cotangent, weight, raw, middle):
            grads = (weight * (raw - middle)).astype(jnp.bfloat16)
            both = dot(grads, keys * jnp.bfloat16(factor), TN)
            return (
                jnp.where(lane_head == 0, both[:tokens], both[tokens:]),
                dot(grads, query),
                dot(weight.astype(jnp.bfloat16), cotangent),
            )

        def joined(sums, new):
            return tuple(a + b for a, b in zip(sums, new))

        def attend(keys, vals, queries, cotangents, offsets, outside=None, final=None):
            query, cotangent = stacked(queries, factor_masks), stacked(cotangents, head_masks)
            scores = dot(keys, query, NT) + offsets
            raw = dot(vals, cotangent, NT)
            top = jnp.max(scores, 0, keepdims=True)
            if outside is not None:
                out_top, out_sum, out_center = (outside[i : i + 1, :] for i in range(3))
                top = jnp.maximum(top, out_top)
            powers = jnp.exp(scores - top)
            total = jnp.sum(powers, 0, keepdims=True)
            middle = jnp.sum(powers * raw, 0, keepdims=True)
            if outside is not None:
                scale = jnp.exp(out_top - top)
                total = total + out_sum * scale
                middle = middle + out_center * scale
            inverse = 1.0 / total
            middle = middle * inverse
            if final is not None:
                for i, row in enumerate((top, inverse, middle)):
                    final[i : i + 1, :] = row
            return products(keys, query, cotangent, powers * inverse, raw, middle)

        def attend_first(pair, keys, vals, offsets):
            query, cotangent = stacked(mine(QU, pair), factor_masks), stacked(mine(None, pair), head_masks)
            scores = dot(keys, query, NT) + offsets
            raw = dot(vals, cotangent, NT)
            top = jnp.max(scores, 0, keepdims=True)
            powers = jnp.exp(scores - top)
            powers_ref[pair, : keys.shape[0], :] = powers
            small[pair, 0:1, :] = top
            small[pair, 1:2, :] = jnp.sum(powers, 0, keepdims=True)
            small[pair, 2:3, :] = jnp.sum(powers * raw, 0, keepdims=True)

        def attend_last(pair, keys, vals):
            query, cotangent = stacked(mine(QU, pair), factor_masks), stacked(mine(None, pair), head_masks)
            top, inverse, middle = (final_in[pair, i : i + 1, :] for i in range(3))
            scale = jnp.exp(small[pair, 0:1, :] - top) * inverse
            raw = dot(vals, cotangent, NT)
            weight = powers_ref[pair, : keys.shape[0], :] * scale
            return products(keys, query, cotangent, weight, raw, middle)

        def put(portion, pair, value):
            gback[portion, :, lanes(pair)] = value.astype(jnp.bfloat16)

        def keep(pair, sums):
            for portion in range(3):
                acc[portion, pair] = sums[portion]

        def mine(kind, pair):
            return up_ref[:, lanes(pair)] if kind is None else own[kind * pairs + pair]

        def local(pair):
            return mine(KE, pair), mine(VA, pair)

        def mine_rows(pair):
            return mine(QU, pair), mine(None, pair)

        def keys_of(pair, count):
            return tuple(keys_in[i, place(pair), : count * tokens, :] for i in range(2))

        def rows_of(pair, slot):
            return tuple(rows_in[i, slot, place(pair)] for i in range(2))

        def contribute(pieces, fresh=False):
            @pl.loop(0, width // COLUMNS)
            def _(c):
                at = pl.ds(pl.multiple_of(c * COLUMNS, COLUMNS), COLUMNS)
                total = None if fresh else part_acc[:, at]
                for portion, some in pieces:
                    cut = slice(some[0] * LANES, (some[-1] + 1) * LANES)
                    term = dot(gback[portion, :, cut], w_ref[portion, at, cut], NT)
                    total = term if total is None else total + term
                part_acc[:, at] = total

        def place_own(some, spot):
            for pair in some:
                for kind in (KE, VA):
                    keys_in[kind - KE, place(pair), block(spot), :] = mine(kind, pair)

        def wait_labels():
            remote(
                labels_in.at[: n_seq - 1], labels_in.at[: n_seq - 1], l_sem.at[0], l_sem.at[1], along[0]
            ).wait_recv()

        if chip == 0:
            for pair in (2, 0, 3, 1):
                for kind in (KE, VA):
                    send_own(0, 2 if pair in high else 1, kind, pair, 0)
                if pair == 2:
                    for copy in label_copies:
                        copy.start()
            make_bias(0, 0, 0, 0)
            for pair in range(pairs):
                sums = attend(*local(pair), *mine_rows(pair), bias[0, :tokens, :])
                put(0, pair, sums[0])
                keep(pair, sums)
            contribute([(0, range(pairs))], True)
            wait_labels()
            make_bias(1, 0, 0, 1)
            for pair in high:
                wait_rows(1, 0, pair, 0)
                statistics(1, 0, pair, 0)
                spot = pairs + place(pair)
                sums = attend(
                    *local(pair), *rows_of(pair, 0), bias[1, :tokens, :],
                    stats_in.at[0, place(pair)], small.at[spot],
                )
                finals(0, 1, pair, 0)
                dq_part(0, 1, pair, 0, sums[0])
                acc[1, pair] += sums[1]
                acc[2, pair] += sums[2]
            for pair in (0, 2, 1, 3):
                dkv_wait(1 if pair in low else 2, pair)
                for kind in (0, 1):
                    put(kind + 1, pair, acc[kind + 1, pair] + dkv_in[kind, pair].astype(jnp.float32))
                contribute([(1, [pair]), (2, [pair])])
        elif chip == 1:
            for kind in (KE, VA):
                send_own(1, 2, kind, 2, 1)
            for kind in (1, 0):
                send_rows(1, 0, kind, 2, 0)
            for copy in label_copies:
                copy.start()
            make_bias(0, 1, 1, 1)
            for pair in high:
                attend_first(pair, *local(pair), bias[0, block(1), :])
                statistics(1, 0, pair, 0)
            for kind in (KE, VA):
                send_own(1, 2, kind, 3, 1)
            for kind in (1, 0):
                send_rows(1, 0, kind, 3, 0)
            place_own(low, 1)
            wait_labels()
            make_bias(0, 0, 0, 1)
            for slot in (0, 1):
                for j in (0, 1):
                    make_bias(1 + slot, j, j, 2 + slot)
            for pair in low:
                wait_keys(0, 1, pair, 0)
                keys = keys_of(pair, 2)
                sums = attend(*keys, *mine_rows(pair), bias[0, : 2 * tokens, :])
                put(0, pair, sums[0])
                for slot in (0, 1):
                    wait_rows(2 + slot, 1, pair, slot)
                    statistics(2 + slot, 1, pair, slot)
                    spot = pairs + slot * middle_pair + pair
                    more = attend(
                        *keys, *rows_of(pair, slot), bias[1 + slot, : 2 * tokens, :],
                        stats_in.at[slot, pair], small.at[spot],
                    )
                    finals(1, 2 + slot, pair, slot)
                    dq_part(1, 2 + slot, pair, slot, more[0])
                    sums = joined(sums, more)
                dkv_send(0, pair, 0, sums)
                for portion in (1, 2):
                    put(portion, pair, sums[portion][block(1)])
            contribute([(portion, low) for portion in range(3)], True)
            for pair in high:
                finals(0, 1, pair, 0)
                keep(pair, attend_last(pair, *local(pair)))
            for pair in high:
                dq_part(0, 1, pair, 0)
                put(0, pair, acc[0, pair] + dq_in[pair].astype(jnp.float32))
            contribute([(0, high)])
            for pair in high:
                dkv_wait(2, pair)
                for kind in (0, 1):
                    put(kind + 1, pair, acc[kind + 1, pair] + dkv_in[kind, pair].astype(jnp.float32))
                contribute([(1, [pair]), (2, [pair])])
        elif chip == 2:
            for pair in low:
                for kind in (KE, VA):
                    send_own(2, 3, kind, pair, 0)
            for copy in label_copies:
                copy.start()
            make_bias(0, 2, 2, 2)
            for pair in low:
                attend_first(pair, *local(pair), bias[0, block(2), :])
                statistics(2, 1, pair, 0)
            for kind in (1, 0):
                send_rows(2, 1, kind, 1, 0)
            place_own(high, 2)
            wait_labels()
            for j in (0, 1):
                make_bias(0, j, j, 2)
            for j in range(3):
                make_bias(1, j, j, 3)
            for pair in high:
                wait_keys(0, 2, pair, 0)
                wait_keys(1, 2, pair, 1)
                keys = keys_of(pair, 3)
                sums = attend(*keys, *mine_rows(pair), bias[0])
                put(0, pair, sums[0])
                wait_rows(3, 2, pair, 0)
                statistics(3, 2, pair, 0)
                more = attend(
                    *keys, *rows_of(pair, 0), bias[1],
                    stats_in.at[0, place(pair)], small.at[pairs + place(pair)],
                )
                finals(2, 3, pair, 0)
                sums = joined(sums, more)
                for j in (0, 1):
                    dkv_send(j, pair, j, sums)
                dq_part(2, 3, pair, 0, more[0])
                for portion in (1, 2):
                    put(portion, pair, sums[portion][block(2)])
            for pair in low:
                finals(1, 2, pair, 0)
                keep(pair, attend_last(pair, *local(pair)))
            contribute([(portion, high) for portion in range(3)], True)
            for pair in low:
                dq_part(1, 2, pair, 0)
                put(0, pair, acc[0, pair] + dq_in[pair].astype(jnp.float32))
            contribute([(0, low)])
            for pair in low:
                dkv_wait(3, pair)
                for kind in (0, 1):
                    put(kind + 1, pair, acc[kind + 1, pair] + dkv_in[kind, pair].astype(jnp.float32))
                contribute([(1, [pair]), (2, [pair])])
        else:
            make_bias(0, 1, 3, 3)
            for pair in high:
                attend_first(pair, *local(pair), bias[0, block(1), :])
                statistics(3, 2, pair, 0)
            for pair, target, slot in ((1, 1, 1), (3, 2, 0)):
                for kind in (1, 0):
                    send_rows(3, target, kind, pair, slot)
            for copy in label_copies:
                copy.start()
            place_own(low, 1)
            wait_labels()
            make_bias(0, 0, 2, 3)
            for pair in low:
                wait_keys(2, 3, pair, 0)
                attend_first(pair, *keys_of(pair, 2), bias[0, : 2 * tokens, :])
                statistics(3, 1, pair, 1)
            for pair in low:
                finals(1, 3, pair, 1)
                sums = attend_last(pair, *keys_of(pair, 2))
                dkv_send(2, pair, 0, sums)
                for portion in (1, 2):
                    put(portion, pair, sums[portion][block(1)])
                acc[0, pair] = sums[0]
            for pair in high:
                finals(2, 3, pair, 0)
                sums = attend_last(pair, *local(pair))
                for portion in (1, 2):
                    put(portion, pair, sums[portion])
                acc[0, pair] = sums[0]
            contribute([(1, range(pairs)), (2, range(pairs))], True)
            for some in (low, high):
                for pair in some:
                    dq_part(1 if pair in low else 2, 3, pair, 1 if pair in low else 0)
                    put(0, pair, acc[0, pair] + dq_in[pair].astype(jnp.float32))
                contribute([(0, some)])
        for at, whole in enumerate((own, own, small)):
            count = started[chip][at]
            remote(
                whole.at[:count], whole.at[:count], t_send.at[at], t_recv.at[0], along[0]
            ).wait_send()

    dispatch(role, range(n_seq))
    assert max(len(n) for n in numbers) <= RECEIVED

    own_cut = pl.ds(pl.multiple_of(core * half, LANES), half)
    half_rows = half // LANES
    exchanges = []
    for c in range(n_head):
        cut = slice(c * half, (c + 1) * half)
        rounded = part_acc[:, cut].astype(jnp.bfloat16)
        part_out[c] = rounded
        exchanges.append(
            remote(
                part_out.at[c], part_in.at[c], h_send.at[c], h_recv.at[c],
                {"head": lax.rem(core + 1, n_head)},
            )
        )
        exchanges[c].start()
        sums = jnp.sum(rounded.astype(jnp.float32) * scaled_ref[:, cut], 0, keepdims=True)
        for i in range(half_rows):
            at = c * half_rows + i
            gain_src[at : at + 1, :] = sums[:, lanes(i)]
    for peer in along:
        remote(gain_src, gain_seq.at[me], s_sem.at[0], s_sem.at[1], peer).start()
    gain_seq[me] = gain_src[...]

    first_sum, second_sum = 0.0, 0.0
    for c in range(n_head):
        cut = slice(c * half, (c + 1) * half)
        exchanges[c].wait_recv()
        gradient = part_out[c].astype(jnp.float32) + part_in[c].astype(jnp.float32)
        scaled_grad = gradient * gain_ref[:, cut]
        first_sum = first_sum + jnp.sum(scaled_grad, -1, keepdims=True)
        second_sum = second_sum + jnp.sum(scaled_grad * scaled_ref[:, cut], -1, keepdims=True)
    gradient = part_out[core].astype(jnp.float32) + part_in[core].astype(jnp.float32)
    inner = gradient * gain_ref[:, own_cut] - first_sum / width
    inner = inner - scaled_ref[:, own_cut] * (second_sum / width)
    grad_ref[...] = (spread_ref[:, :1] * inner).astype(jnp.bfloat16)

    all_seq = gain_seq.at[: n_seq - 1]
    over_seq = remote(all_seq, all_seq, s_sem.at[0], s_sem.at[1], along[0])
    over_seq.wait_recv()
    total = gain_seq[0]
    for j in range(1, n_seq):
        total = total + gain_seq[j]
    gain_mid[...] = total
    slot = group * n_head + core
    for peer in across:
        remote(gain_mid, gain_all.at[slot], d_sem.at[0], d_sem.at[1], peer).start()
    gain_all[slot] = total
    for copy in exchanges:
        copy.wait_send()
    over_seq.wait_send()
    all_labels = labels_in.at[: n_seq - 1]
    remote(all_labels, all_labels, l_sem.at[0], l_sem.at[1], along[0]).wait_send()
    all_rest = gain_all.at[: n_dp * n_head - 1]
    over_rest = remote(all_rest, all_rest, d_sem.at[0], d_sem.at[1], across[0])
    over_rest.wait_recv()
    total = gain_all[0]
    for j in range(1, n_dp * n_head):
        total = total + gain_all[j]
    gain_sum[...] = total * total_rows ** (-0.5)
    for i in range(half_rows):
        gain_out_ref[:, lanes(i)] = gain_sum[pl.ds(core * half_rows + i, 1), :]
    over_rest.wait_send()


def hand_on(gradient_in, gain_in, gradient_out, gain_out):
    gradient_out[...] = gradient_in[...]
    gain_out[...] = gain_in[...]


def on_device_heads(hidden, norm_gain, projection, upstream, cluster):
    n_seq, n_head, n_dp = (lax.axis_size(a) for a in ("seq", "head", "dp"))
    tokens, width = hidden.shape[1:]
    spans = projection.shape[2]
    pairs = spans // LANES
    half = width // n_head
    wide = 2 * tokens
    gain_rows = width // LANES
    vmem = pl.BlockSpec(memory_space=pltpu.VMEM)
    hbm = pl.BlockSpec(memory_space=pl.ANY)
    dma = pltpu.SemaphoreType.DMA
    bf16, f32 = jnp.bfloat16, jnp.float32
    results = (
        jax.ShapeDtypeStruct((tokens, half), bf16),
        jax.ShapeDtypeStruct((1, half), f32),
    )
    gradient, gain = pl.pallas_call(
        functools.partial(fused, n_seq, n_head, n_dp, n_seq * n_dp * tokens),
        out_shape=results,
        in_specs=[hbm] * 5,
        out_specs=(vmem, vmem),
        scratch_shapes=[
            pltpu.VMEM((tokens, width), bf16),
            pltpu.VMEM((1, width), f32),
            pltpu.VMEM((1, tokens), jnp.int32),
            pltpu.VMEM((3, width, spans), bf16),
            pltpu.VMEM((tokens, width), f32),
            pltpu.VMEM((tokens, spans), bf16),
            pltpu.VMEM((3 * pairs, tokens, LANES), bf16),
            pltpu.VMEM((2, pairs // 2, 3 * tokens, LANES), bf16),
            pltpu.VMEM((2, 2, pairs // 2, tokens, LANES), bf16),
            pltpu.VMEM((8, wide), f32),
            pltpu.VMEM((n_seq, 8, wide), f32),
            pltpu.VMEM((3, 3 * tokens, wide), f32),
            pltpu.VMEM((pairs, 2 * tokens, wide), f32),
            pltpu.VMEM((2 * pairs, 8, wide), f32),
            pltpu.VMEM((2, pairs // 2, 8, wide), f32),
            pltpu.VMEM((pairs, 8, wide), f32),
            pltpu.VMEM((2, pairs // 2, tokens, LANES), bf16),
            pltpu.VMEM((pairs, tokens, LANES), bf16),
            pltpu.VMEM((2, pairs // 2, 2, tokens, LANES), bf16),
            pltpu.VMEM((2, pairs, tokens, LANES), bf16),
            pltpu.VMEM((3, pairs, tokens, LANES), f32),
            pltpu.VMEM((3, tokens, spans), bf16),
            pltpu.VMEM((tokens, width), f32),
            pltpu.VMEM((n_head, tokens, half), bf16),
            pltpu.VMEM((n_head, tokens, half), bf16),
            pltpu.VMEM((tokens, LANES), f32),
            pltpu.VMEM((gain_rows, LANES), f32),
            pltpu.VMEM((n_seq, gain_rows, LANES), f32),
            pltpu.VMEM((gain_rows, LANES), f32),
            pltpu.VMEM((n_dp * n_head, gain_rows, LANES), f32),
            pltpu.VMEM((gain_rows, LANES), f32),
            dma((4,)),
            dma((3,)),
            dma((3,)),
            dma((RECEIVED,)),
            dma((2,)),
            dma((n_head,)),
            dma((n_head,)),
            dma((2,)),
            dma((2,)),
        ],
        compiler_params=pltpu.CompilerParams(collective_id=0, has_side_effects=True),
    )(hidden[0], norm_gain[None, :], projection, upstream[0], cluster[:, :, 0])
    gradient, gain = pl.pallas_call(
        hand_on, out_shape=results, in_specs=[vmem] * 2, out_specs=(vmem, vmem)
    )(gradient, gain)
    return (gradient.reshape(1, tokens, half), gain.reshape(half))


def splits_by_heads(mesh, hidden, projection):
    n_seq, n_head, n_dp = (mesh.shape[a] for a in ("seq", "head", "dp"))
    tokens = hidden.shape[1] // n_seq
    return (
        n_head == 2
        and n_dp > 1
        and n_seq == 4
        and LANES == 2 * HDIM
        and CLUS_DEV * n_seq <= 16
        and projection.shape[2] // n_head == 4 * LANES
        and hidden.shape[2] % (n_head * COLUMNS) == 0
        and tokens % (LANES // 2) == 0
        and tokens <= 2 * LANES
    )


def solution(mesh):
    in_specs = (
        P("dp", "seq", None),
        P(),
        P(None, None, "head"),
        P("dp", "seq", "head"),
        P("dp", "seq", None),
    )
    out_specs = (P("dp", "seq", "head"), P("head"))

    def program(hidden, norm_gain, projection, upstream, cluster):
        body = on_device_heads if splits_by_heads(mesh, hidden, projection) else on_device
        return jax.shard_map(
            body, mesh=mesh, in_specs=in_specs, out_specs=out_specs, check_vma=False
        )(hidden, norm_gain, projection, upstream, cluster)

    return program
```

```python
import functools

import jax
import jax.numpy as jnp
from jax import lax
from jax.experimental import pallas as pl
from jax.experimental.pallas import tpu as pltpu
from jax.sharding import PartitionSpec as P

HDIM = 64
CLUS_DEV = 1


epsilon = 1e-05
masked = -1e30


def normalize(values, norm_gain):
    values = values.astype(jnp.float32)
    center = values - jnp.mean(values, -1, keepdims=True)
    spread = lax.rsqrt(jnp.mean(center * center, -1, keepdims=True) + epsilon)
    scaled = center * spread
    return (scaled, spread, (scaled * norm_gain).astype(jnp.bfloat16))


def attend_backward(queries, key_rows, values, upstream, allowed, factor):
    scores = (
        lax.dot_general(
            queries, key_rows, (((1,), (1,)), ((), ())), preferred_element_type=jnp.float32
        )
        * factor
    )
    scores = jnp.where(allowed, scores, masked)
    powers = jnp.exp(scores - jnp.max(scores, -1, keepdims=True))
    weights = powers / jnp.sum(powers, -1, keepdims=True)
    rounded = weights.astype(jnp.bfloat16)
    output = jnp.dot(rounded, values, preferred_element_type=jnp.float32)
    center_term = jnp.sum(upstream.astype(jnp.float32) * output, -1, keepdims=True)
    grad_values = lax.dot_general(
        rounded, upstream, (((0,), (0,)), ((), ())), preferred_element_type=jnp.float32
    ).astype(jnp.bfloat16)
    grad_weights = lax.dot_general(
        upstream, values, (((1,), (1,)), ((), ())), preferred_element_type=jnp.float32
    )
    grad_scores = (weights * (grad_weights - center_term) * factor).astype(jnp.bfloat16)
    grad_queries = jnp.dot(grad_scores, key_rows, preferred_element_type=jnp.float32).astype(
        jnp.bfloat16
    )
    grad_keys = lax.dot_general(
        grad_scores, queries, (((0,), (0,)), ((), ())), preferred_element_type=jnp.float32
    ).astype(jnp.bfloat16)
    return (grad_queries, grad_keys, grad_values)


def cluster_grads(payload, validity, head_width):
    row_count = payload.shape[0]
    spans = payload.shape[1] // 4
    heads_local = spans // head_width
    positions = lax.broadcasted_iota(jnp.int32, (row_count, row_count), 0)
    others = lax.broadcasted_iota(jnp.int32, (row_count, row_count), 1)
    allowed = (positions >= others) & (validity[None, :] > 0)
    factor = head_width ** (-0.5)

    def one_head(head_index, result):
        offset = head_index * head_width

        def select(portion):
            return lax.dynamic_slice_in_dim(payload, portion * spans + offset, head_width, 1)

        grads_head = attend_backward(select(0), select(1), select(2), select(3), allowed, factor)
        for portion in range(3):
            result = lax.dynamic_update_slice_in_dim(
                result, grads_head[portion], portion * spans + offset, 1
            )
        return result

    return lax.fori_loop(0, heads_local, one_head, jnp.zeros((row_count, 3 * spans), jnp.bfloat16))


def on_device(hidden, norm_gain, projection, upstream, cluster):
    seq_count = lax.axis_size("seq")
    tokens = hidden.shape[1]
    width_model = hidden.shape[2]
    spans = projection.shape[2]
    clusters_all = CLUS_DEV * seq_count
    slot_rows = 3 * tokens // clusters_all
    scaled, spread, normed = normalize(hidden[0], norm_gain)
    labels = cluster[0, :, 0]
    member = (labels[:, None] == jnp.arange(clusters_all, dtype=jnp.int32)[None, :]).astype(
        jnp.int32
    )
    ranks = jnp.sum(jnp.cumsum(member, 0) * member, 1) - 1
    target = labels * slot_rows + ranks
    projected = jnp.einsum(
        "td,kdh->tkh", normed, projection, preferred_element_type=jnp.float32
    ).astype(jnp.bfloat16)
    payload = jnp.concatenate([projected.reshape(tokens, 3 * spans), upstream[0]], 1)
    columns = payload.shape[1]
    outgoing = jnp.zeros((clusters_all * slot_rows, columns), jnp.bfloat16).at[target].set(payload)
    outgoing = outgoing.reshape(seq_count, CLUS_DEV, slot_rows, columns)
    present = jnp.zeros((clusters_all * slot_rows,), jnp.bfloat16).at[target].set(1.0)
    present = present.reshape(seq_count, CLUS_DEV, slot_rows)
    rows_in = lax.all_to_all(outgoing, "seq", split_axis=0, concat_axis=0, tiled=True)
    marks_in = lax.all_to_all(present, "seq", split_axis=0, concat_axis=0, tiled=True)
    sources = rows_in.shape[0]
    item_count = rows_in.shape[1]
    stacked = jnp.swapaxes(rows_in, 0, 1).reshape(item_count, sources * slot_rows, rows_in.shape[3])
    mark_rows = jnp.swapaxes(marks_in, 0, 1).reshape(item_count, sources * slot_rows)

    def per_item(entries):
        return cluster_grads(entries[0], entries[1].astype(jnp.float32), HDIM)

    results = lax.map(per_item, (stacked, mark_rows))
    results = jnp.einsum(
        "irkh,kdh->ird",
        results.reshape(item_count, sources * slot_rows, 3, spans),
        projection,
        preferred_element_type=jnp.float32,
    ).astype(jnp.bfloat16)
    width_out = results.shape[-1]
    results = results.reshape(item_count, sources, slot_rows, width_out)
    answer = jnp.swapaxes(results, 0, 1)
    returned = lax.all_to_all(answer, "seq", split_axis=0, concat_axis=0, tiled=True)
    restored = returned.reshape(clusters_all * slot_rows, width_model)[target]
    partial_value = restored.astype(jnp.float32)
    half_width = width_model // lax.axis_size("head")
    offset = lax.axis_index("head") * half_width
    own_scaled = lax.dynamic_slice_in_dim(scaled, offset, half_width, 1)
    own_gain = lax.dynamic_slice_in_dim(norm_gain, offset, half_width, 0)
    gradient = lax.psum_scatter(
        partial_value.astype(jnp.bfloat16), "head", scatter_dimension=1, tiled=True
    ).astype(jnp.float32)
    scaled_grad = gradient * own_gain
    first_sum, second_sum = lax.psum(
        (
            jnp.sum(scaled_grad, -1, keepdims=True),
            jnp.sum(scaled_grad * own_scaled, -1, keepdims=True),
        ),
        "head",
    )
    first_mean = first_sum / width_model
    second_mean = second_sum / width_model
    input_gradient = (spread * (scaled_grad - first_mean - own_scaled * second_mean)).astype(
        jnp.bfloat16
    )
    local_sum = jnp.sum(gradient * own_scaled, 0)
    gain_total = lax.psum(local_sum, ("seq", "dp"))
    gain_gradient = gain_total * (seq_count * lax.axis_size("dp") * tokens) ** (-0.5)
    return (input_gradient.reshape(1, tokens, half_width), gain_gradient)


MESH = pl.DeviceIdType.MESH
LANES = 128
RECEIVED = 16
COLUMNS = 256
QU, KE, VA = range(3)
NT = (((1,), (1,)), ((), ()))
TN = (((0,), (0,)), ((), ()))


def dot(left, right, dims=(((1,), (0,)), ((), ()))):
    return lax.dot_general(left, right, dims, preferred_element_type=jnp.float32)


def fused(
    n_seq, n_head, n_dp, total_rows,
    hidden_hbm, gain_hbm, proj_hbm, up_hbm, cluster_hbm,
    grad_ref, gain_out_ref,
    hidden_ref, gain_ref, cluster_ref, w_ref, scaled_ref, up_ref, own, keys_in, rows_in,
    labels_out, labels_in, bias, powers_ref, small, stats_in, final_in,
    dq_out, dq_in, dkv_out, dkv_in, acc, gback,
    part_acc, part_out, part_in, spread_ref, gain_src, gain_all,
    in_sem, w_sem, t_send, t_recv, l_sem, h_send, h_recv, d_sem,
):
    me = lax.axis_index("seq")
    core = lax.axis_index("head")
    group = lax.axis_index("dp")
    tokens, width = hidden_hbm.shape
    pairs = up_hbm.shape[1] // LANES
    half = width // n_head
    factor = HDIM ** (-0.5)
    middle_pair = pairs // 2
    low, high = range(middle_pair), range(middle_pair, pairs)

    barrier = pltpu.get_barrier_semaphore()
    along = [{"seq": lax.rem(me + o, n_seq)} for o in range(1, n_seq)]
    across = [
        {"dp": lax.rem(group + o // n_head, n_dp), "head": lax.rem(core + o % n_head, n_head)}
        for o in range(1, n_dp * n_head)
    ]
    for peer in along + across:
        pl.semaphore_signal(barrier, inc=1, device_id=peer, device_id_type=MESH)

    upper = lax.div(me, n_seq // 2)
    load_up = pltpu.make_async_copy(up_hbm, up_ref, in_sem.at[0])
    load_hidden = pltpu.make_async_copy(hidden_hbm, hidden_ref, in_sem.at[1])
    load_gain = pltpu.make_async_copy(gain_hbm, gain_ref, in_sem.at[2])
    load_cluster = pltpu.make_async_copy(cluster_hbm, cluster_ref, in_sem.at[3])
    order = [lax.rem(1 - upper + i, 3) for i in range(3)]
    w_copies = [pltpu.make_async_copy(proj_hbm.at[p], w_ref.at[p], w_sem.at[p]) for p in order]
    for copy in (load_cluster, load_up, load_hidden, load_gain, *w_copies):
        copy.start()

    def remote(src, dst, send, recv, peer):
        return pltpu.make_async_remote_copy(
            src_ref=src, dst_ref=dst, send_sem=send, recv_sem=recv,
            device_id=peer, device_id_type=MESH,
        )

    def lanes(pair):
        return slice(pair * LANES, (pair + 1) * LANES)

    def block(j):
        return slice(j * tokens, (j + 1) * tokens)

    def place(pair):
        return pair % middle_pair

    numbers = [{} for _ in range(n_seq)]
    started = [[0, 0, 0] for _ in range(n_seq)]

    def transfer(key, src, dst, target, group_at):
        at = numbers[target].setdefault(key, len(numbers[target]))
        return remote(
            src, dst, t_send.at[group_at], t_recv.at[at], {"seq": jnp.int32(target)}
        )

    def send(source, key, src, dst, target, group_at):
        started[source][group_at] += 1
        transfer((source, *key), src, dst, target, group_at).start()

    def wait(source, target, key, dst):
        transfer((source, *key), dst, dst, target, 0).wait_recv()

    def send_own(source, target, kind, pair, spot):
        dst = keys_in.at[kind - KE, place(pair), block(spot)]
        send(source, ("keys", pair), own.at[kind * pairs + pair], dst, target, 0)

    def wait_keys(source, target, pair, spot):
        wait(source, target, ("keys", pair), keys_in.at[:, place(pair), block(spot)])

    def send_rows(source, target, kind, pair, slot):
        src = up_ref.at[:, lanes(pair)] if kind == 1 else own.at[QU * pairs + pair]
        send(source, ("rows", pair), src, rows_in.at[kind, slot, place(pair)], target, 0)

    def wait_rows(source, target, pair, slot):
        wait(source, target, ("rows", pair), rows_in.at[:, slot, place(pair)])

    def dispatch(stage, chips):
        for chip in chips:
            pl.when(me == chip)(functools.partial(stage, chip))

    def send_early(chip):
        for pair, target, slot in ((0, 1, chip - 2), (2, 2, 0))[: chip - 1]:
            send_rows(chip, target, 1, pair, slot)

    def send_queries(chip):
        for pair, target, slot in ((0, 1, chip - 2), (2, 2, 0))[: chip - 1]:
            send_rows(chip, target, 0, pair, slot)

    load_cluster.wait()
    labels = cluster_ref[...].astype(jnp.float32)
    labels = jnp.concatenate([labels, labels], 1)
    labels_out[...] = jnp.zeros_like(labels_out)
    labels_out[:1, :] = labels

    def enter():
        pl.semaphore_wait(barrier, len(along) + len(across))
        for peer in along:
            remote(labels_out, labels_in.at[me], l_sem.at[0], l_sem.at[1], peer).start()

    pl.when(upper == 1)(enter)
    load_up.wait()
    dispatch(send_early, (2, 3))

    load_hidden.wait()
    load_gain.wait()
    values = hidden_ref[...].astype(jnp.float32)
    center = values - jnp.mean(values, -1, keepdims=True)
    spread = lax.rsqrt(jnp.mean(center * center, -1, keepdims=True) + epsilon)
    scaled = center * spread
    scaled_ref[...] = scaled
    spread_ref[...] = jnp.broadcast_to(spread, spread_ref.shape)
    normed = (scaled * gain_ref[...]).astype(jnp.bfloat16)
    for i, p in enumerate(order):
        w_copies[i].wait()
        made = dot(normed, w_ref[p]).astype(jnp.bfloat16)
        for j in range(pairs):
            own[p * pairs + j] = made[:, lanes(j)]
        if i == 0:
            dispatch(send_queries, (2, 3))
    small[...] = jnp.zeros_like(small)

    pl.when(upper == 0)(enter)

    lane_head = lax.broadcasted_iota(jnp.int32, (1, LANES), 1) // HDIM
    head_masks = [jnp.where(lane_head == h, 1.0, 0.0).astype(jnp.bfloat16) for h in range(2)]
    factor_masks = [mask * jnp.bfloat16(factor) for mask in head_masks]

    def stacked(rows, masks):
        return jnp.concatenate([rows * mask for mask in masks], 0)

    def role(chip):
        def statistics(source, target, pair, slot):
            dst = stats_in.at[slot, place(pair)]
            if source == chip:
                send(chip, ("stats", pair), small.at[pair], dst, target, 2)
            else:
                wait(source, chip, ("stats", pair), dst)

        def finals(source, target, pair, slot):
            if source == chip:
                src = small.at[pairs + slot * middle_pair + place(pair)]
                send(chip, ("final", pair), src, final_in.at[pair], target, 2)
            else:
                wait(source, chip, ("final", pair), final_in.at[pair])

        def dq_part(source, target, pair, slot, value=None):
            if source == chip:
                dq_out[slot, place(pair)] = value.astype(jnp.bfloat16)
                send(chip, ("dq", pair), dq_out.at[slot, place(pair)], dq_in.at[pair], target, 1)
            else:
                wait(source, chip, ("dq", pair), dq_in.at[pair])

        def dkv_send(target, pair, spot, sums):
            for kind in (1, 0):
                dkv_out[kind, place(pair), spot] = sums[kind + 1][block(spot)].astype(jnp.bfloat16)
                src = dkv_out.at[kind, place(pair), spot]
                send(chip, ("dkv", pair), src, dkv_in.at[kind, pair], target, 1)

        def dkv_wait(source, pair):
            wait(source, chip, ("dkv", pair), dkv_in.at[:, pair])

        def one_hot(j):
            row = labels_out[:1, :] if j == chip else labels_in[j, :1, :]
            classes = lax.broadcasted_iota(jnp.int32, (16, 2 * tokens), 0).astype(jnp.float32)
            return jnp.where(classes == row, 1.0, 0.0).astype(jnp.bfloat16)

        def make_bias(slot, spot, j, row):
            allowed = dot(one_hot(j)[:, :tokens], one_hot(row), TN) > 0.5
            if j == row:
                key_at = lax.broadcasted_iota(jnp.int32, (tokens, 2 * tokens), 0)
                row_at = lax.broadcasted_iota(jnp.int32, (tokens, 2 * tokens), 1)
                row_at = jnp.where(row_at >= tokens, row_at - tokens, row_at)
                allowed = allowed & (key_at <= row_at)
            bias[slot, block(spot), :] = jnp.where(allowed, 0.0, masked)

        def products(keys, query, cotangent, weight, raw, middle):
            grads = (weight * (raw - middle)).astype(jnp.bfloat16)
            both = dot(grads, keys * jnp.bfloat16(factor), TN)
            return (
                jnp.where(lane_head == 0, both[:tokens], both[tokens:]),
                dot(grads, query),
                dot(weight.astype(jnp.bfloat16), cotangent),
            )

        def joined(sums, new):
            return tuple(a + b for a, b in zip(sums, new))

        def attend(keys, vals, queries, cotangents, offsets, outside=None, final=None):
            query, cotangent = stacked(queries, factor_masks), stacked(cotangents, head_masks)
            scores = dot(keys, query, NT) + offsets
            raw = dot(vals, cotangent, NT)
            top = jnp.max(scores, 0, keepdims=True)
            if outside is not None:
                out_top, out_sum, out_center = (outside[i : i + 1, :] for i in range(3))
                top = jnp.maximum(top, out_top)
            powers = jnp.exp(scores - top)
            total = jnp.sum(powers, 0, keepdims=True)
            middle = jnp.sum(powers * raw, 0, keepdims=True)
            if outside is not None:
                scale = jnp.exp(out_top - top)
                total = total + out_sum * scale
                middle = middle + out_center * scale
            inverse = 1.0 / total
            middle = middle * inverse
            if final is not None:
                for i, row in enumerate((top, inverse, middle)):
                    final[i : i + 1, :] = row
            return products(keys, query, cotangent, powers * inverse, raw, middle)

        def attend_first(pair, keys, vals, offsets):
            query, cotangent = stacked(mine(QU, pair), factor_masks), stacked(mine(None, pair), head_masks)
            scores = dot(keys, query, NT) + offsets
            raw = dot(vals, cotangent, NT)
            top = jnp.max(scores, 0, keepdims=True)
            powers = jnp.exp(scores - top)
            powers_ref[pair, : keys.shape[0], :] = powers
            small[pair, 0:1, :] = top
            small[pair, 1:2, :] = jnp.sum(powers, 0, keepdims=True)
            small[pair, 2:3, :] = jnp.sum(powers * raw, 0, keepdims=True)

        def attend_last(pair, keys, vals):
            query, cotangent = stacked(mine(QU, pair), factor_masks), stacked(mine(None, pair), head_masks)
            top, inverse, middle = (final_in[pair, i : i + 1, :] for i in range(3))
            scale = jnp.exp(small[pair, 0:1, :] - top) * inverse
            raw = dot(vals, cotangent, NT)
            weight = powers_ref[pair, : keys.shape[0], :] * scale
            return products(keys, query, cotangent, weight, raw, middle)

        def put(portion, pair, value):
            gback[portion, :, lanes(pair)] = value.astype(jnp.bfloat16)

        def keep(pair, sums):
            for portion in range(3):
                acc[portion, pair] = sums[portion]

        def mine(kind, pair):
            return up_ref[:, lanes(pair)] if kind is None else own[kind * pairs + pair]

        def local(pair):
            return mine(KE, pair), mine(VA, pair)

        def mine_rows(pair):
            return mine(QU, pair), mine(None, pair)

        def keys_of(pair, count):
            return tuple(keys_in[i, place(pair), : count * tokens, :] for i in range(2))

        def rows_of(pair, slot):
            return tuple(rows_in[i, slot, place(pair)] for i in range(2))

        def contribute(pieces, fresh=False):
            left, right = [], []
            for portion, some in pieces:
                cut = slice(some[0] * LANES, (some[-1] + 1) * LANES)
                left.append(gback[portion, :, cut])
                right.append(w_ref[portion, :, cut])
            total = dot(jnp.concatenate(left, 1), jnp.concatenate(right, 1), NT)
            part_acc[...] = total if fresh else part_acc[...] + total

        def place_own(some, spot):
            for pair in some:
                for kind in (KE, VA):
                    keys_in[kind - KE, place(pair), block(spot), :] = mine(kind, pair)

        def wait_labels():
            remote(
                labels_in.at[: n_seq - 1], labels_in.at[: n_seq - 1], l_sem.at[0], l_sem.at[1], along[0]
            ).wait_recv()

        if chip == 0:
            for pair in (2, 0, 3, 1):
                for kind in (KE, VA):
                    send_own(0, 2 if pair in high else 1, kind, pair, 0)
            make_bias(0, 0, 0, 0)
            for pair in range(pairs):
                sums = attend(*local(pair), *mine_rows(pair), bias[0, :tokens, :])
                put(0, pair, sums[0])
                keep(pair, sums)
            contribute([(0, range(pairs))], True)
            wait_labels()
            make_bias(1, 0, 0, 1)
            for pair in high:
                wait_rows(1, 0, pair, 0)
                statistics(1, 0, pair, 0)
                spot = pairs + place(pair)
                sums = attend(
                    *local(pair), *rows_of(pair, 0), bias[1, :tokens, :],
                    stats_in.at[0, place(pair)], small.at[spot],
                )
                finals(0, 1, pair, 0)
                dq_part(0, 1, pair, 0, sums[0])
                acc[1, pair] += sums[1]
                acc[2, pair] += sums[2]
            for pair in (0, 2, 1, 3):
                dkv_wait(1 if pair in low else 2, pair)
                for kind in (0, 1):
                    put(kind + 1, pair, acc[kind + 1, pair] + dkv_in[kind, pair].astype(jnp.float32))
                contribute([(1, [pair]), (2, [pair])])
        elif chip == 1:
            for kind in (KE, VA):
                send_own(1, 2, kind, 2, 1)
            for kind in (1, 0):
                send_rows(1, 0, kind, 2, 0)
            make_bias(0, 1, 1, 1)
            for pair in high:
                attend_first(pair, *local(pair), bias[0, block(1), :])
                statistics(1, 0, pair, 0)
            for kind in (KE, VA):
                send_own(1, 2, kind, 3, 1)
            for kind in (1, 0):
                send_rows(1, 0, kind, 3, 0)
            place_own(low, 1)
            wait_labels()
            make_bias(0, 0, 0, 1)
            for slot in (0, 1):
                for j in (0, 1):
                    make_bias(1 + slot, j, j, 2 + slot)
            for pair in low:
                wait_keys(0, 1, pair, 0)
                keys = keys_of(pair, 2)
                sums = attend(*keys, *mine_rows(pair), bias[0, : 2 * tokens, :])
                put(0, pair, sums[0])
                for slot in (0, 1):
                    wait_rows(2 + slot, 1, pair, slot)
                    statistics(2 + slot, 1, pair, slot)
                    spot = pairs + slot * middle_pair + pair
                    more = attend(
                        *keys, *rows_of(pair, slot), bias[1 + slot, : 2 * tokens, :],
                        stats_in.at[slot, pair], small.at[spot],
                    )
                    finals(1, 2 + slot, pair, slot)
                    dq_part(1, 2 + slot, pair, slot, more[0])
                    sums = joined(sums, more)
                dkv_send(0, pair, 0, sums)
                for portion in (1, 2):
                    put(portion, pair, sums[portion][block(1)])
            contribute([(portion, low) for portion in range(3)], True)
            for pair in high:
                finals(0, 1, pair, 0)
                keep(pair, attend_last(pair, *local(pair)))
            for pair in high:
                dq_part(0, 1, pair, 0)
                put(0, pair, acc[0, pair] + dq_in[pair].astype(jnp.float32))
            contribute([(0, high)])
            for pair in high:
                dkv_wait(2, pair)
                for kind in (0, 1):
                    put(kind + 1, pair, acc[kind + 1, pair] + dkv_in[kind, pair].astype(jnp.float32))
                contribute([(1, [pair]), (2, [pair])])
        elif chip == 2:
            for pair in low:
                for kind in (KE, VA):
                    send_own(2, 3, kind, pair, 0)
            make_bias(0, 2, 2, 2)
            for pair in low:
                attend_first(pair, *local(pair), bias[0, block(2), :])
                statistics(2, 1, pair, 0)
            for kind in (1, 0):
                send_rows(2, 1, kind, 1, 0)
            place_own(high, 2)
            wait_labels()
            for j in (0, 1):
                make_bias(0, j, j, 2)
            for j in range(3):
                make_bias(1, j, j, 3)
            for pair in high:
                wait_keys(0, 2, pair, 0)
                wait_keys(1, 2, pair, 1)
                keys = keys_of(pair, 3)
                sums = attend(*keys, *mine_rows(pair), bias[0])
                put(0, pair, sums[0])
                wait_rows(3, 2, pair, 0)
                statistics(3, 2, pair, 0)
                more = attend(
                    *keys, *rows_of(pair, 0), bias[1],
                    stats_in.at[0, place(pair)], small.at[pairs + place(pair)],
                )
                finals(2, 3, pair, 0)
                sums = joined(sums, more)
                for j in (0, 1):
                    dkv_send(j, pair, j, sums)
                dq_part(2, 3, pair, 0, more[0])
                for portion in (1, 2):
                    put(portion, pair, sums[portion][block(2)])
            for pair in low:
                finals(1, 2, pair, 0)
                keep(pair, attend_last(pair, *local(pair)))
            contribute([(portion, high) for portion in range(3)], True)
            for pair in low:
                dq_part(1, 2, pair, 0)
                put(0, pair, acc[0, pair] + dq_in[pair].astype(jnp.float32))
            contribute([(0, low)])
            for pair in low:
                dkv_wait(3, pair)
                for kind in (0, 1):
                    put(kind + 1, pair, acc[kind + 1, pair] + dkv_in[kind, pair].astype(jnp.float32))
                contribute([(1, [pair]), (2, [pair])])
        else:
            make_bias(0, 1, 3, 3)
            for pair in high:
                attend_first(pair, *local(pair), bias[0, block(1), :])
                statistics(3, 2, pair, 0)
            for pair, target, slot in ((1, 1, 1), (3, 2, 0)):
                for kind in (1, 0):
                    send_rows(3, target, kind, pair, slot)
            place_own(low, 1)
            wait_labels()
            make_bias(0, 0, 2, 3)
            for pair in low:
                wait_keys(2, 3, pair, 0)
                attend_first(pair, *keys_of(pair, 2), bias[0, : 2 * tokens, :])
                statistics(3, 1, pair, 1)
            for pair in low:
                finals(1, 3, pair, 1)
                sums = attend_last(pair, *keys_of(pair, 2))
                dkv_send(2, pair, 0, sums)
                for portion in (1, 2):
                    put(portion, pair, sums[portion][block(1)])
                acc[0, pair] = sums[0]
            for pair in high:
                finals(2, 3, pair, 0)
                sums = attend_last(pair, *local(pair))
                for portion in (1, 2):
                    put(portion, pair, sums[portion])
                acc[0, pair] = sums[0]
            contribute([(1, range(pairs)), (2, range(pairs))], True)
            for some in (low, high):
                for pair in some:
                    dq_part(1 if pair in low else 2, 3, pair, 1 if pair in low else 0)
                    put(0, pair, acc[0, pair] + dq_in[pair].astype(jnp.float32))
                contribute([(0, some)])
        for at, whole in enumerate((own, own, small)):
            count = started[chip][at]
            remote(
                whole.at[:count], whole.at[:count], t_send.at[at], t_recv.at[0], along[0]
            ).wait_send()

    dispatch(role, range(n_seq))
    assert max(len(n) for n in numbers) <= RECEIVED

    own_cut = pl.ds(pl.multiple_of(core * half, LANES), half)
    exchanges = []
    for c in range(n_head):
        cut = slice(c * half, (c + 1) * half)
        rounded = part_acc[:, cut].astype(jnp.bfloat16)
        part_out[c] = rounded
        exchanges.append(
            remote(
                part_out.at[c], part_in.at[c], h_send.at[c], h_recv.at[c],
                {"head": lax.rem(core + 1, n_head)},
            )
        )
        exchanges[c].start()
        sums = jnp.sum(rounded.astype(jnp.float32) * scaled_ref[:, cut], 0, keepdims=True)
        gain_src[c] = sums
    slot = (me * n_dp + group) * n_head + core
    for o in range(1, n_seq * n_dp * n_head):
        peer = {
            "seq": lax.rem(me + o // (n_dp * n_head), n_seq),
            "dp": lax.rem(group + o // n_head % n_dp, n_dp),
            "head": lax.rem(core + o % n_head, n_head),
        }
        src = gain_src.at[peer["head"]]
        remote(src, gain_all.at[slot], d_sem.at[0], d_sem.at[1], peer).start()
    gain_all[slot] = gain_src[core]

    first_sum, second_sum = 0.0, 0.0
    for c in range(n_head):
        cut = slice(c * half, (c + 1) * half)
        exchanges[c].wait_recv()
        gradient = part_out[c].astype(jnp.float32) + part_in[c].astype(jnp.float32)
        scaled_grad = gradient * gain_ref[:, cut]
        first_sum = first_sum + jnp.sum(scaled_grad, -1, keepdims=True)
        second_sum = second_sum + jnp.sum(scaled_grad * scaled_ref[:, cut], -1, keepdims=True)
    gradient = part_out[core].astype(jnp.float32) + part_in[core].astype(jnp.float32)
    inner = gradient * gain_ref[:, own_cut] - first_sum / width
    inner = inner - scaled_ref[:, own_cut] * (second_sum / width)
    grad_ref[...] = (spread_ref[:, :1] * inner).astype(jnp.bfloat16)

    for copy in exchanges:
        copy.wait_send()
    all_labels = labels_in.at[: n_seq - 1]
    remote(all_labels, all_labels, l_sem.at[0], l_sem.at[1], along[0]).wait_send()
    all_gains = gain_all.at[: n_seq * n_dp * n_head - 1]
    over_all = remote(all_gains, all_gains, d_sem.at[0], d_sem.at[1], along[0])
    over_all.wait_recv()
    gain_out_ref[...] = jnp.sum(gain_all[...], 0) * total_rows ** (-0.5)
    over_all.wait_send()


def hand_on(gradient_in, gain_in, gradient_out, gain_out):
    gradient_out[...] = gradient_in[...]
    gain_out[...] = gain_in[...]


def on_device_heads(hidden, norm_gain, projection, upstream, cluster):
    n_seq, n_head, n_dp = (lax.axis_size(a) for a in ("seq", "head", "dp"))
    tokens, width = hidden.shape[1:]
    spans = projection.shape[2]
    pairs = spans // LANES
    half = width // n_head
    wide = 2 * tokens
    vmem = pl.BlockSpec(memory_space=pltpu.VMEM)
    hbm = pl.BlockSpec(memory_space=pl.ANY)
    dma = pltpu.SemaphoreType.DMA
    bf16, f32 = jnp.bfloat16, jnp.float32
    results = (
        jax.ShapeDtypeStruct((tokens, half), bf16),
        jax.ShapeDtypeStruct((1, half), f32),
    )
    gradient, gain = pl.pallas_call(
        functools.partial(fused, n_seq, n_head, n_dp, n_seq * n_dp * tokens),
        out_shape=results,
        in_specs=[hbm] * 5,
        out_specs=(vmem, vmem),
        scratch_shapes=[
            pltpu.VMEM((tokens, width), bf16),
            pltpu.VMEM((1, width), f32),
            pltpu.VMEM((1, tokens), jnp.int32),
            pltpu.VMEM((3, width, spans), bf16),
            pltpu.VMEM((tokens, width), f32),
            pltpu.VMEM((tokens, spans), bf16),
            pltpu.VMEM((3 * pairs, tokens, LANES), bf16),
            pltpu.VMEM((2, pairs // 2, 3 * tokens, LANES), bf16),
            pltpu.VMEM((2, 2, pairs // 2, tokens, LANES), bf16),
            pltpu.VMEM((8, wide), f32),
            pltpu.VMEM((n_seq, 8, wide), f32),
            pltpu.VMEM((3, 3 * tokens, wide), f32),
            pltpu.VMEM((pairs, 2 * tokens, wide), f32),
            pltpu.VMEM((2 * pairs, 8, wide), f32),
            pltpu.VMEM((2, pairs // 2, 8, wide), f32),
            pltpu.VMEM((pairs, 8, wide), f32),
            pltpu.VMEM((2, pairs // 2, tokens, LANES), bf16),
            pltpu.VMEM((pairs, tokens, LANES), bf16),
            pltpu.VMEM((2, pairs // 2, 2, tokens, LANES), bf16),
            pltpu.VMEM((2, pairs, tokens, LANES), bf16),
            pltpu.VMEM((3, pairs, tokens, LANES), f32),
            pltpu.VMEM((3, tokens, spans), bf16),
            pltpu.VMEM((tokens, width), f32),
            pltpu.VMEM((n_head, tokens, half), bf16),
            pltpu.VMEM((n_head, tokens, half), bf16),
            pltpu.VMEM((tokens, LANES), f32),
            pltpu.VMEM((n_head, 1, half), f32),
            pltpu.VMEM((n_seq * n_dp * n_head, 1, half), f32),
            dma((4,)),
            dma((3,)),
            dma((3,)),
            dma((RECEIVED,)),
            dma((2,)),
            dma((n_head,)),
            dma((n_head,)),
            dma((2,)),
        ],
        compiler_params=pltpu.CompilerParams(collective_id=0, has_side_effects=True),
    )(hidden[0], norm_gain[None, :], projection, upstream[0], cluster[:, :, 0])
    gradient, gain = pl.pallas_call(
        hand_on, out_shape=results, in_specs=[vmem] * 2, out_specs=(vmem, vmem)
    )(gradient, gain)
    return (gradient.reshape(1, tokens, half), gain.reshape(half))


def splits_by_heads(mesh, hidden, projection):
    n_seq, n_head, n_dp = (mesh.shape[a] for a in ("seq", "head", "dp"))
    tokens = hidden.shape[1] // n_seq
    return (
        n_head == 2
        and n_dp > 1
        and n_seq == 4
        and LANES == 2 * HDIM
        and CLUS_DEV * n_seq <= 16
        and projection.shape[2] // n_head == 4 * LANES
        and hidden.shape[2] % (n_head * COLUMNS) == 0
        and tokens % (LANES // 2) == 0
        and tokens <= 2 * LANES
    )


def solution(mesh):
    in_specs = (
        P("dp", "seq", None),
        P(),
        P(None, None, "head"),
        P("dp", "seq", "head"),
        P("dp", "seq", None),
    )
    out_specs = (P("dp", "seq", "head"), P("head"))

    def program(hidden, norm_gain, projection, upstream, cluster):
        body = on_device_heads if splits_by_heads(mesh, hidden, projection) else on_device
        return jax.shard_map(
            body, mesh=mesh, in_specs=in_specs, out_specs=out_specs, check_vma=False
        )(hidden, norm_gain, projection, upstream, cluster)

    return program
```

```python
import functools

import jax
import jax.numpy as jnp
from jax import lax
from jax.experimental import pallas as pl
from jax.experimental.pallas import tpu as pltpu
from jax.sharding import PartitionSpec as P

HDIM = 64
CLUS_DEV = 1


epsilon = 1e-05
masked = -1e30


def normalize(values, norm_gain):
    values = values.astype(jnp.float32)
    center = values - jnp.mean(values, -1, keepdims=True)
    spread = lax.rsqrt(jnp.mean(center * center, -1, keepdims=True) + epsilon)
    scaled = center * spread
    return (scaled, spread, (scaled * norm_gain).astype(jnp.bfloat16))


def attend_backward(queries, key_rows, values, upstream, allowed, factor):
    scores = (
        lax.dot_general(
            queries, key_rows, (((1,), (1,)), ((), ())), preferred_element_type=jnp.float32
        )
        * factor
    )
    scores = jnp.where(allowed, scores, masked)
    powers = jnp.exp(scores - jnp.max(scores, -1, keepdims=True))
    weights = powers / jnp.sum(powers, -1, keepdims=True)
    rounded = weights.astype(jnp.bfloat16)
    output = jnp.dot(rounded, values, preferred_element_type=jnp.float32)
    center_term = jnp.sum(upstream.astype(jnp.float32) * output, -1, keepdims=True)
    grad_values = lax.dot_general(
        rounded, upstream, (((0,), (0,)), ((), ())), preferred_element_type=jnp.float32
    ).astype(jnp.bfloat16)
    grad_weights = lax.dot_general(
        upstream, values, (((1,), (1,)), ((), ())), preferred_element_type=jnp.float32
    )
    grad_scores = (weights * (grad_weights - center_term) * factor).astype(jnp.bfloat16)
    grad_queries = jnp.dot(grad_scores, key_rows, preferred_element_type=jnp.float32).astype(
        jnp.bfloat16
    )
    grad_keys = lax.dot_general(
        grad_scores, queries, (((0,), (0,)), ((), ())), preferred_element_type=jnp.float32
    ).astype(jnp.bfloat16)
    return (grad_queries, grad_keys, grad_values)


def cluster_grads(payload, validity, head_width):
    row_count = payload.shape[0]
    spans = payload.shape[1] // 4
    heads_local = spans // head_width
    positions = lax.broadcasted_iota(jnp.int32, (row_count, row_count), 0)
    others = lax.broadcasted_iota(jnp.int32, (row_count, row_count), 1)
    allowed = (positions >= others) & (validity[None, :] > 0)
    factor = head_width ** (-0.5)

    def one_head(head_index, result):
        offset = head_index * head_width

        def select(portion):
            return lax.dynamic_slice_in_dim(payload, portion * spans + offset, head_width, 1)

        grads_head = attend_backward(select(0), select(1), select(2), select(3), allowed, factor)
        for portion in range(3):
            result = lax.dynamic_update_slice_in_dim(
                result, grads_head[portion], portion * spans + offset, 1
            )
        return result

    return lax.fori_loop(0, heads_local, one_head, jnp.zeros((row_count, 3 * spans), jnp.bfloat16))


def on_device(hidden, norm_gain, projection, upstream, cluster):
    seq_count = lax.axis_size("seq")
    tokens = hidden.shape[1]
    width_model = hidden.shape[2]
    spans = projection.shape[2]
    clusters_all = CLUS_DEV * seq_count
    slot_rows = 3 * tokens // clusters_all
    scaled, spread, normed = normalize(hidden[0], norm_gain)
    labels = cluster[0, :, 0]
    member = (labels[:, None] == jnp.arange(clusters_all, dtype=jnp.int32)[None, :]).astype(
        jnp.int32
    )
    ranks = jnp.sum(jnp.cumsum(member, 0) * member, 1) - 1
    target = labels * slot_rows + ranks
    projected = jnp.einsum(
        "td,kdh->tkh", normed, projection, preferred_element_type=jnp.float32
    ).astype(jnp.bfloat16)
    payload = jnp.concatenate([projected.reshape(tokens, 3 * spans), upstream[0]], 1)
    columns = payload.shape[1]
    outgoing = jnp.zeros((clusters_all * slot_rows, columns), jnp.bfloat16).at[target].set(payload)
    outgoing = outgoing.reshape(seq_count, CLUS_DEV, slot_rows, columns)
    present = jnp.zeros((clusters_all * slot_rows,), jnp.bfloat16).at[target].set(1.0)
    present = present.reshape(seq_count, CLUS_DEV, slot_rows)
    rows_in = lax.all_to_all(outgoing, "seq", split_axis=0, concat_axis=0, tiled=True)
    marks_in = lax.all_to_all(present, "seq", split_axis=0, concat_axis=0, tiled=True)
    sources = rows_in.shape[0]
    item_count = rows_in.shape[1]
    stacked = jnp.swapaxes(rows_in, 0, 1).reshape(item_count, sources * slot_rows, rows_in.shape[3])
    mark_rows = jnp.swapaxes(marks_in, 0, 1).reshape(item_count, sources * slot_rows)

    def per_item(entries):
        return cluster_grads(entries[0], entries[1].astype(jnp.float32), HDIM)

    results = lax.map(per_item, (stacked, mark_rows))
    results = jnp.einsum(
        "irkh,kdh->ird",
        results.reshape(item_count, sources * slot_rows, 3, spans),
        projection,
        preferred_element_type=jnp.float32,
    ).astype(jnp.bfloat16)
    width_out = results.shape[-1]
    results = results.reshape(item_count, sources, slot_rows, width_out)
    answer = jnp.swapaxes(results, 0, 1)
    returned = lax.all_to_all(answer, "seq", split_axis=0, concat_axis=0, tiled=True)
    restored = returned.reshape(clusters_all * slot_rows, width_model)[target]
    partial_value = restored.astype(jnp.float32)
    half_width = width_model // lax.axis_size("head")
    offset = lax.axis_index("head") * half_width
    own_scaled = lax.dynamic_slice_in_dim(scaled, offset, half_width, 1)
    own_gain = lax.dynamic_slice_in_dim(norm_gain, offset, half_width, 0)
    gradient = lax.psum_scatter(
        partial_value.astype(jnp.bfloat16), "head", scatter_dimension=1, tiled=True
    ).astype(jnp.float32)
    scaled_grad = gradient * own_gain
    first_sum, second_sum = lax.psum(
        (
            jnp.sum(scaled_grad, -1, keepdims=True),
            jnp.sum(scaled_grad * own_scaled, -1, keepdims=True),
        ),
        "head",
    )
    first_mean = first_sum / width_model
    second_mean = second_sum / width_model
    input_gradient = (spread * (scaled_grad - first_mean - own_scaled * second_mean)).astype(
        jnp.bfloat16
    )
    local_sum = jnp.sum(gradient * own_scaled, 0)
    gain_total = lax.psum(local_sum, ("seq", "dp"))
    gain_gradient = gain_total * (seq_count * lax.axis_size("dp") * tokens) ** (-0.5)
    return (input_gradient.reshape(1, tokens, half_width), gain_gradient)


MESH = pl.DeviceIdType.MESH
LANES = 128
RECEIVED = 16
COLUMNS = 256
QU, KE, VA = range(3)
NT = (((1,), (1,)), ((), ()))
TN = (((0,), (0,)), ((), ()))


def dot(left, right, dims=(((1,), (0,)), ((), ()))):
    return lax.dot_general(left, right, dims, preferred_element_type=jnp.float32)


def fused(
    n_seq, n_head, n_dp, total_rows,
    hidden_hbm, gain_hbm, proj_hbm, up_hbm, cluster_hbm,
    grad_ref, gain_out_ref,
    hidden_ref, gain_ref, cluster_ref, w_ref, scaled_ref, up_ref, own, keys_in, rows_in,
    labels_out, labels_in, bias, powers_ref, small, stats_in, final_in,
    dq_out, dq_in, dkv_out, dkv_in, acc, gback,
    part_acc, part_out, part_in, spread_ref, gain_src, gain_all,
    in_sem, w_sem, t_send, t_recv, l_sem, h_send, h_recv, d_sem,
):
    me = lax.axis_index("seq")
    core = lax.axis_index("head")
    group = lax.axis_index("dp")
    tokens, width = hidden_hbm.shape
    pairs = up_hbm.shape[1] // LANES
    half = width // n_head
    factor = HDIM ** (-0.5)
    middle_pair = pairs // 2
    low, high = range(middle_pair), range(middle_pair, pairs)

    barrier = pltpu.get_barrier_semaphore()
    along = [{"seq": lax.rem(me + o, n_seq)} for o in range(1, n_seq)]
    across = [
        {"dp": lax.rem(group + o // n_head, n_dp), "head": lax.rem(core + o % n_head, n_head)}
        for o in range(1, n_dp * n_head)
    ]
    for peer in along + across:
        pl.semaphore_signal(barrier, inc=1, device_id=peer, device_id_type=MESH)

    upper = lax.div(me, n_seq // 2)
    load_up = pltpu.make_async_copy(up_hbm, up_ref, in_sem.at[0])
    load_hidden = pltpu.make_async_copy(hidden_hbm, hidden_ref, in_sem.at[1])
    load_gain = pltpu.make_async_copy(gain_hbm, gain_ref, in_sem.at[2])
    load_cluster = pltpu.make_async_copy(cluster_hbm, cluster_ref, in_sem.at[3])
    order = [lax.rem(1 - upper + i, 3) for i in range(3)]
    w_copies = [pltpu.make_async_copy(proj_hbm.at[p], w_ref.at[p], w_sem.at[p]) for p in order]
    for copy in (load_cluster, load_up, load_hidden, load_gain, *w_copies):
        copy.start()

    def remote(src, dst, send, recv, peer):
        return pltpu.make_async_remote_copy(
            src_ref=src, dst_ref=dst, send_sem=send, recv_sem=recv,
            device_id=peer, device_id_type=MESH,
        )

    def lanes(pair):
        return slice(pair * LANES, (pair + 1) * LANES)

    def block(j):
        return slice(j * tokens, (j + 1) * tokens)

    def place(pair):
        return pair % middle_pair

    numbers = [{} for _ in range(n_seq)]
    started = [[0, 0, 0] for _ in range(n_seq)]

    def transfer(key, src, dst, target, group_at):
        at = numbers[target].setdefault(key, len(numbers[target]))
        return remote(
            src, dst, t_send.at[group_at], t_recv.at[at], {"seq": jnp.int32(target)}
        )

    def send(source, key, src, dst, target, group_at):
        started[source][group_at] += 1
        transfer((source, *key), src, dst, target, group_at).start()

    def wait(source, target, key, dst):
        transfer((source, *key), dst, dst, target, 0).wait_recv()

    def send_own(source, target, kind, pair, spot):
        dst = keys_in.at[kind - KE, place(pair), block(spot)]
        send(source, ("keys", pair), own.at[kind * pairs + pair], dst, target, 0)

    def wait_keys(source, target, pair, spot):
        wait(source, target, ("keys", pair), keys_in.at[:, place(pair), block(spot)])

    def send_rows(source, target, kind, pair, slot):
        src = up_ref.at[:, lanes(pair)] if kind == 1 else own.at[QU * pairs + pair]
        send(source, ("rows", pair), src, rows_in.at[kind, slot, place(pair)], target, 0)

    def wait_rows(source, target, pair, slot):
        wait(source, target, ("rows", pair), rows_in.at[:, slot, place(pair)])

    def dispatch(stage, chips):
        for chip in chips:
            pl.when(me == chip)(functools.partial(stage, chip))

    def send_early(chip):
        for pair, target, slot in ((0, 1, chip - 2), (2, 2, 0))[: chip - 1]:
            send_rows(chip, target, 1, pair, slot)

    def send_queries(chip):
        for pair, target, slot in ((0, 1, chip - 2), (2, 2, 0))[: chip - 1]:
            send_rows(chip, target, 0, pair, slot)

    load_cluster.wait()
    labels = cluster_ref[...].astype(jnp.float32)
    labels = jnp.concatenate([labels, labels], 1)
    labels_out[...] = labels

    def enter():
        pl.semaphore_wait(barrier, len(along) + len(across))
        for peer in along:
            remote(labels_out, labels_in.at[me], l_sem.at[0], l_sem.at[1], peer).start()

    pl.when(upper == 1)(enter)
    load_up.wait()
    dispatch(send_early, (2, 3))

    load_hidden.wait()
    load_gain.wait()
    values = hidden_ref[...].astype(jnp.float32)
    center = values - jnp.mean(values, -1, keepdims=True)
    spread = lax.rsqrt(jnp.mean(center * center, -1, keepdims=True) + epsilon)
    scaled = center * spread
    scaled_ref[...] = scaled
    spread_ref[...] = jnp.broadcast_to(spread, spread_ref.shape)
    normed = (scaled * gain_ref[...]).astype(jnp.bfloat16)
    for i, p in enumerate(order):
        w_copies[i].wait()
        made = dot(normed, w_ref[p]).astype(jnp.bfloat16)
        for j in range(pairs):
            own[p * pairs + j] = made[:, lanes(j)]
        if i == 0:
            dispatch(send_queries, (2, 3))
    pl.when(upper == 0)(enter)

    lane_head = lax.broadcasted_iota(jnp.int32, (1, LANES), 1) // HDIM
    head_masks = [jnp.where(lane_head == h, 1.0, 0.0).astype(jnp.bfloat16) for h in range(2)]
    factor_masks = [mask * jnp.bfloat16(factor) for mask in head_masks]

    def stacked(rows, masks):
        return jnp.concatenate([rows * mask for mask in masks], 0)

    def role(chip):
        def statistics(source, target, pair, slot):
            dst = stats_in.at[slot, place(pair), :3, :]
            if source == chip:
                send(chip, ("stats", pair), small.at[pair, :3, :], dst, target, 2)
            else:
                wait(source, chip, ("stats", pair), dst)

        def finals(source, target, pair, slot):
            if source == chip:
                src = small.at[pairs + slot * middle_pair + place(pair), :3, :]
                send(chip, ("final", pair), src, final_in.at[pair, :3, :], target, 2)
            else:
                wait(source, chip, ("final", pair), final_in.at[pair, :3, :])

        def exchange(owner, pair, slot):
            finals(chip, owner, pair, slot)
            statistics(owner, chip, pair, slot)
            return stats_in.at[slot, place(pair)]

        def dq_part(source, target, pair, slot, value=None):
            if source == chip:
                dq_out[slot, place(pair)] = value.astype(jnp.bfloat16)
                send(chip, ("dq", pair), dq_out.at[slot, place(pair)], dq_in.at[pair], target, 1)
            else:
                wait(source, chip, ("dq", pair), dq_in.at[pair])

        def dkv_send(target, pair, spot, sums):
            for kind in (1, 0):
                dkv_out[kind, place(pair), spot] = sums[kind + 1][block(spot)].astype(jnp.bfloat16)
                src = dkv_out.at[kind, place(pair), spot]
                send(chip, ("dkv", pair), src, dkv_in.at[kind, pair], target, 1)

        def dkv_wait(source, pair):
            wait(source, chip, ("dkv", pair), dkv_in.at[:, pair])

        def one_hot(j):
            row = labels_out[...] if j == chip else labels_in[j]
            classes = lax.broadcasted_iota(jnp.int32, (16, 2 * tokens), 0).astype(jnp.float32)
            return jnp.where(classes == row, 1.0, 0.0).astype(jnp.bfloat16)

        def make_bias(slot, spot, j, row):
            allowed = dot(one_hot(j)[:, :tokens], one_hot(row), TN) > 0.5
            if j == row:
                key_at = lax.broadcasted_iota(jnp.int32, (tokens, 2 * tokens), 0)
                row_at = lax.broadcasted_iota(jnp.int32, (tokens, 2 * tokens), 1)
                row_at = jnp.where(row_at >= tokens, row_at - tokens, row_at)
                allowed = allowed & (key_at <= row_at)
            bias[slot, block(spot), :] = jnp.where(allowed, 0.0, masked)

        def products(keys, query, cotangent, weight, raw, middle):
            grads = (weight * (raw - middle)).astype(jnp.bfloat16)
            both = dot(grads, keys * jnp.bfloat16(factor), TN)
            return (
                jnp.where(lane_head == 0, both[:tokens], both[tokens:]),
                dot(grads, query),
                dot(weight.astype(jnp.bfloat16), cotangent),
            )

        def joined(sums, new):
            return tuple(a + b for a, b in zip(sums, new))

        def begin(keys, vals, query, cotangent, offsets):
            scores = dot(keys, query, NT) + offsets
            raw = dot(vals, cotangent, NT)
            top = jnp.max(scores, 0, keepdims=True)
            powers = jnp.exp(scores - top)
            total = jnp.sum(powers, 0, keepdims=True)
            return powers, raw, (top, total, jnp.sum(powers * raw, 0, keepdims=True))

        def meet(ours, theirs):
            top = jnp.maximum(ours[0], theirs[0])
            scale, other = jnp.exp(ours[0] - top), jnp.exp(theirs[0] - top)
            inverse = 1.0 / (ours[1] * scale + theirs[1] * other)
            return scale * inverse, (ours[2] * scale + theirs[2] * other) * inverse

        def read(ref):
            return tuple(ref[i : i + 1, :] for i in range(3))

        def write(ref, rows):
            for i, row in enumerate(rows):
                ref[i : i + 1, :] = row

        def attend(keys, vals, queries, cotangents, offsets, local_at=None, exchange=None):
            query, cotangent = stacked(queries, factor_masks), stacked(cotangents, head_masks)
            powers, raw, ours = begin(keys, vals, query, cotangent, offsets)
            if exchange is None:
                scale = 1.0 / ours[1]
                middle = ours[2] * scale
            else:
                write(small.at[local_at], ours)
                scale, middle = meet(ours, read(exchange()))
            return products(keys, query, cotangent, powers * scale, raw, middle)

        def attend_first(pair, at, keys, vals, rows, offsets):
            query, cotangent = stacked(rows[0], factor_masks), stacked(rows[1], head_masks)
            powers, _, ours = begin(keys, vals, query, cotangent, offsets)
            powers_ref[pair, : keys.shape[0], :] = powers
            write(small.at[at], ours)

        def attend_last(pair, at, theirs, keys, vals, rows):
            query, cotangent = stacked(rows[0], factor_masks), stacked(rows[1], head_masks)
            scale, middle = meet(read(small.at[at]), read(theirs))
            raw = dot(vals, cotangent, NT)
            return products(
                keys, query, cotangent, powers_ref[pair, : keys.shape[0], :] * scale, raw, middle
            )

        def own_last(pair, keys, vals):
            return attend_last(pair, pair, final_in.at[pair], keys, vals, mine_rows(pair))

        def put(portion, pair, value):
            gback[portion, :, lanes(pair)] = value.astype(jnp.bfloat16)

        def keep(pair, sums):
            for portion in range(3):
                acc[portion, pair] = sums[portion]

        def mine(kind, pair):
            return up_ref[:, lanes(pair)] if kind is None else own[kind * pairs + pair]

        def local(pair):
            return mine(KE, pair), mine(VA, pair)

        def mine_rows(pair):
            return mine(QU, pair), mine(None, pair)

        def keys_of(pair, count):
            return tuple(keys_in[i, place(pair), : count * tokens, :] for i in range(2))

        def rows_of(pair, slot):
            return tuple(rows_in[i, slot, place(pair)] for i in range(2))

        def contribute(pieces, fresh=False):
            left, right = [], []
            for portion, some in pieces:
                cut = slice(some[0] * LANES, (some[-1] + 1) * LANES)
                left.append(gback[portion, :, cut])
                right.append(w_ref[portion, :, cut])
            total = dot(jnp.concatenate(left, 1), jnp.concatenate(right, 1), NT)
            part_acc[...] = total if fresh else part_acc[...] + total

        def place_own(some, spot):
            for pair in some:
                for kind in (KE, VA):
                    keys_in[kind - KE, place(pair), block(spot), :] = mine(kind, pair)

        def wait_labels():
            remote(
                labels_in.at[: n_seq - 1], labels_in.at[: n_seq - 1], l_sem.at[0], l_sem.at[1], along[0]
            ).wait_recv()

        if chip == 0:
            def send_keys(some):
                for pair in some:
                    for kind in (KE, VA):
                        send_own(0, 2 if pair in high else 1, kind, pair, 0)

            send_keys((0, 2))
            make_bias(0, 0, 0, 0)
            for pair in range(pairs):
                sums = attend(*local(pair), *mine_rows(pair), bias[0, :tokens, :])
                put(0, pair, sums[0])
                keep(pair, sums)
            send_keys((3, 1))
            contribute([(0, range(pairs))], True)
            wait_labels()
            make_bias(1, 0, 0, 1)
            for pair in high:
                wait_rows(1, 0, pair, 0)
                sums = attend(
                    *local(pair), *rows_of(pair, 0), bias[1, :tokens, :],
                    pairs + place(pair), functools.partial(exchange, 1, pair, 0),
                )
                dq_part(0, 1, pair, 0, sums[0])
                acc[1, pair] += sums[1]
                acc[2, pair] += sums[2]
            for pair in (0, 2, 1, 3):
                dkv_wait(1 if pair in low else 2, pair)
                for kind in (0, 1):
                    put(kind + 1, pair, acc[kind + 1, pair] + dkv_in[kind, pair].astype(jnp.float32))
                contribute([(1, [pair]), (2, [pair])])
        elif chip == 1:
            for kind in (KE, VA):
                send_own(1, 2, kind, 2, 1)
            for kind in (1, 0):
                send_rows(1, 0, kind, 2, 0)
            make_bias(0, 1, 1, 1)
            for pair in high:
                attend_first(pair, pair, *local(pair), mine_rows(pair), bias[0, block(1), :])
                statistics(1, 0, pair, 0)
            place_own(low, 1)
            wait_labels()
            for kind in (KE, VA):
                send_own(1, 2, kind, 3, 1)
            for kind in (1, 0):
                send_rows(1, 0, kind, 3, 0)
            make_bias(0, 0, 0, 1)
            for slot in (0, 1):
                for j in (0, 1):
                    make_bias(1 + slot, j, j, 2 + slot)
            for pair in low:
                wait_keys(0, 1, pair, 0)
                keys = keys_of(pair, 2)
                wait_rows(3, 1, pair, 1)
                attend_first(
                    pair, pairs + middle_pair + pair, *keys, rows_of(pair, 1), bias[2, : 2 * tokens, :]
                )
                finals(1, 3, pair, 1)
                sums = attend(*keys, *mine_rows(pair), bias[0, : 2 * tokens, :])
                put(0, pair, sums[0])
                wait_rows(2, 1, pair, 0)
                more = attend(
                    *keys, *rows_of(pair, 0), bias[1, : 2 * tokens, :],
                    pairs + pair, functools.partial(exchange, 2, pair, 0),
                )
                dq_part(1, 2, pair, 0, more[0])
                sums = joined(sums, more)
                statistics(3, 1, pair, 1)
                more = attend_last(
                    pair, pairs + middle_pair + pair, stats_in.at[1, pair], *keys, rows_of(pair, 1)
                )
                sums = joined(sums, more)
                dkv_send(0, pair, 0, sums)
                dq_part(1, 3, pair, 1, more[0])
                for portion in (1, 2):
                    put(portion, pair, sums[portion][block(1)])
            contribute([(portion, low) for portion in range(3)], True)
            for pair in high:
                finals(0, 1, pair, 0)
                keep(pair, own_last(pair, *local(pair)))
            for pair in high:
                dq_part(0, 1, pair, 0)
                put(0, pair, acc[0, pair] + dq_in[pair].astype(jnp.float32))
            contribute([(0, high)])
            for pair in high:
                dkv_wait(2, pair)
                for kind in (0, 1):
                    put(kind + 1, pair, acc[kind + 1, pair] + dkv_in[kind, pair].astype(jnp.float32))
                contribute([(1, [pair]), (2, [pair])])
        elif chip == 2:
            for kind in (KE, VA):
                send_own(2, 3, kind, 0, 0)
            make_bias(0, 2, 2, 2)
            for pair in low:
                attend_first(pair, pair, *local(pair), mine_rows(pair), bias[0, block(2), :])
                statistics(2, 1, pair, 0)
            place_own(high, 2)
            wait_labels()
            for kind in (1, 0):
                send_rows(2, 1, kind, 1, 0)
            for kind in (KE, VA):
                send_own(2, 3, kind, 1, 0)
            for j in (0, 1):
                make_bias(0, j, j, 2)
            for j in range(3):
                make_bias(1, j, j, 3)
            for pair in high:
                wait_keys(0, 2, pair, 0)
                wait_keys(1, 2, pair, 1)
                keys = keys_of(pair, 3)
                sums = attend(*keys, *mine_rows(pair), bias[0])
                put(0, pair, sums[0])
                wait_rows(3, 2, pair, 0)
                more = attend(
                    *keys, *rows_of(pair, 0), bias[1],
                    pairs + place(pair), functools.partial(exchange, 3, pair, 0),
                )
                sums = joined(sums, more)
                for j in (0, 1):
                    dkv_send(j, pair, j, sums)
                dq_part(2, 3, pair, 0, more[0])
                for portion in (1, 2):
                    put(portion, pair, sums[portion][block(2)])
            for pair in low:
                finals(1, 2, pair, 0)
                keep(pair, own_last(pair, *local(pair)))
            contribute([(portion, high) for portion in range(3)], True)
            for pair in low:
                dq_part(1, 2, pair, 0)
                put(0, pair, acc[0, pair] + dq_in[pair].astype(jnp.float32))
            contribute([(0, low)])
            for pair in low:
                dkv_wait(3, pair)
                for kind in (0, 1):
                    put(kind + 1, pair, acc[kind + 1, pair] + dkv_in[kind, pair].astype(jnp.float32))
                contribute([(1, [pair]), (2, [pair])])
        else:
            make_bias(0, 1, 3, 3)
            for pair in high:
                attend_first(pair, pair, *local(pair), mine_rows(pair), bias[0, block(1), :])
                statistics(3, 2, pair, 0)
            for kind in (1, 0):
                send_rows(3, 1, kind, 1, 1)
            place_own(low, 1)
            wait_labels()
            make_bias(0, 0, 2, 3)
            for pair in low:
                wait_keys(2, 3, pair, 0)
                attend_first(pair, pair, *keys_of(pair, 2), mine_rows(pair), bias[0, : 2 * tokens, :])
                statistics(3, 1, pair, 1)
                if pair == 0:
                    for kind in (1, 0):
                        send_rows(3, 2, kind, 3, 0)
            for pair in low:
                finals(1, 3, pair, 1)
                sums = own_last(pair, *keys_of(pair, 2))
                dkv_send(2, pair, 0, sums)
                for portion in (1, 2):
                    put(portion, pair, sums[portion][block(1)])
                acc[0, pair] = sums[0]
            for pair in high:
                finals(2, 3, pair, 0)
                sums = own_last(pair, *local(pair))
                for portion in (1, 2):
                    put(portion, pair, sums[portion])
                acc[0, pair] = sums[0]
            contribute([(1, range(pairs)), (2, range(pairs))], True)
            for some in (low, high):
                for pair in some:
                    dq_part(1 if pair in low else 2, 3, pair, 1 if pair in low else 0)
                    put(0, pair, acc[0, pair] + dq_in[pair].astype(jnp.float32))
                contribute([(0, some)])
        for at, whole in enumerate((own, own, small)):
            sent = whole.at[: started[chip][at]]
            sent = sent.at[:, :3, :] if at == 2 else sent
            remote(
                sent, sent, t_send.at[at], t_recv.at[0], along[0]
            ).wait_send()

    dispatch(role, range(n_seq))
    assert max(len(n) for n in numbers) <= RECEIVED

    own_cut = pl.ds(pl.multiple_of(core * half, LANES), half)
    exchanges = []
    for c in range(n_head):
        cut = slice(c * half, (c + 1) * half)
        rounded = part_acc[:, cut].astype(jnp.bfloat16)
        part_out[c] = rounded
        exchanges.append(
            remote(
                part_out.at[c], part_in.at[c], h_send.at[c], h_recv.at[c],
                {"head": lax.rem(core + 1, n_head)},
            )
        )
        exchanges[c].start()
        sums = jnp.sum(rounded.astype(jnp.float32) * scaled_ref[:, cut], 0, keepdims=True)
        gain_src[c] = sums
    slot = (me * n_dp + group) * n_head + core
    for o in range(1, n_seq * n_dp * n_head):
        peer = {
            "seq": lax.rem(me + o // (n_dp * n_head), n_seq),
            "dp": lax.rem(group + o // n_head % n_dp, n_dp),
            "head": lax.rem(core + o % n_head, n_head),
        }
        src = gain_src.at[peer["head"]]
        remote(src, gain_all.at[slot], d_sem.at[0], d_sem.at[1], peer).start()
    gain_all[slot] = gain_src[core]

    first_sum, second_sum = 0.0, 0.0
    for c in range(n_head):
        cut = slice(c * half, (c + 1) * half)
        exchanges[c].wait_recv()
        gradient = part_out[c].astype(jnp.float32) + part_in[c].astype(jnp.float32)
        scaled_grad = gradient * gain_ref[:, cut]
        first_sum = first_sum + jnp.sum(scaled_grad, -1, keepdims=True)
        second_sum = second_sum + jnp.sum(scaled_grad * scaled_ref[:, cut], -1, keepdims=True)
    gradient = part_out[core].astype(jnp.float32) + part_in[core].astype(jnp.float32)
    inner = gradient * gain_ref[:, own_cut] - first_sum / width
    inner = inner - scaled_ref[:, own_cut] * (second_sum / width)
    grad_ref[...] = (spread_ref[:, :1] * inner).astype(jnp.bfloat16)

    for copy in exchanges:
        copy.wait_send()
    all_labels = labels_in.at[: n_seq - 1]
    remote(all_labels, all_labels, l_sem.at[0], l_sem.at[1], along[0]).wait_send()
    all_gains = gain_all.at[: n_seq * n_dp * n_head - 1]
    over_all = remote(all_gains, all_gains, d_sem.at[0], d_sem.at[1], along[0])
    over_all.wait_recv()
    gain_out_ref[...] = jnp.sum(gain_all[...], 0) * total_rows ** (-0.5)
    over_all.wait_send()


def hand_on(gradient_in, gain_in, gradient_out, gain_out):
    gradient_out[...] = gradient_in[...]
    gain_out[...] = gain_in[...]


def on_device_heads(hidden, norm_gain, projection, upstream, cluster):
    n_seq, n_head, n_dp = (lax.axis_size(a) for a in ("seq", "head", "dp"))
    tokens, width = hidden.shape[1:]
    spans = projection.shape[2]
    pairs = spans // LANES
    half = width // n_head
    wide = 2 * tokens
    vmem = pl.BlockSpec(memory_space=pltpu.VMEM)
    hbm = pl.BlockSpec(memory_space=pl.ANY)
    dma = pltpu.SemaphoreType.DMA
    bf16, f32 = jnp.bfloat16, jnp.float32
    results = (
        jax.ShapeDtypeStruct((tokens, half), bf16),
        jax.ShapeDtypeStruct((1, half), f32),
    )
    gradient, gain = pl.pallas_call(
        functools.partial(fused, n_seq, n_head, n_dp, n_seq * n_dp * tokens),
        out_shape=results,
        in_specs=[hbm] * 5,
        out_specs=(vmem, vmem),
        scratch_shapes=[
            pltpu.VMEM((tokens, width), bf16),
            pltpu.VMEM((1, width), f32),
            pltpu.VMEM((1, tokens), jnp.int32),
            pltpu.VMEM((3, width, spans), bf16),
            pltpu.VMEM((tokens, width), f32),
            pltpu.VMEM((tokens, spans), bf16),
            pltpu.VMEM((3 * pairs, tokens, LANES), bf16),
            pltpu.VMEM((2, pairs // 2, 3 * tokens, LANES), bf16),
            pltpu.VMEM((2, 2, pairs // 2, tokens, LANES), bf16),
            pltpu.VMEM((1, wide), f32),
            pltpu.VMEM((n_seq, 1, wide), f32),
            pltpu.VMEM((3, 3 * tokens, wide), f32),
            pltpu.VMEM((pairs, 2 * tokens, wide), f32),
            pltpu.VMEM((2 * pairs, 8, wide), f32),
            pltpu.VMEM((2, pairs // 2, 8, wide), f32),
            pltpu.VMEM((pairs, 8, wide), f32),
            pltpu.VMEM((2, pairs // 2, tokens, LANES), bf16),
            pltpu.VMEM((pairs, tokens, LANES), bf16),
            pltpu.VMEM((2, pairs // 2, 2, tokens, LANES), bf16),
            pltpu.VMEM((2, pairs, tokens, LANES), bf16),
            pltpu.VMEM((3, pairs, tokens, LANES), f32),
            pltpu.VMEM((3, tokens, spans), bf16),
            pltpu.VMEM((tokens, width), f32),
            pltpu.VMEM((n_head, tokens, half), bf16),
            pltpu.VMEM((n_head, tokens, half), bf16),
            pltpu.VMEM((tokens, LANES), f32),
            pltpu.VMEM((n_head, 1, half), f32),
            pltpu.VMEM((n_seq * n_dp * n_head, 1, half), f32),
            dma((4,)),
            dma((3,)),
            dma((3,)),
            dma((RECEIVED,)),
            dma((2,)),
            dma((n_head,)),
            dma((n_head,)),
            dma((2,)),
        ],
        compiler_params=pltpu.CompilerParams(
            collective_id=0, has_side_effects=True, vmem_limit_bytes=24 << 20
        ),
    )(*(
        pltpu.with_memory_space_constraint(array, pltpu.HBM)
        for array in (hidden[0], norm_gain[None, :], projection, upstream[0], cluster[:, :, 0])
    ))
    gradient, gain = pl.pallas_call(
        hand_on,
        out_shape=results,
        in_specs=[vmem] * 2,
        out_specs=(vmem, vmem),
        compiler_params=pltpu.CompilerParams(vmem_limit_bytes=4 << 20),
    )(gradient, gain)
    return (gradient.reshape(1, tokens, half), gain.reshape(half))


def splits_by_heads(mesh, hidden, projection):
    n_seq, n_head, n_dp = (mesh.shape[a] for a in ("seq", "head", "dp"))
    tokens = hidden.shape[1] // n_seq
    return (
        n_head == 2
        and n_dp > 1
        and n_seq == 4
        and LANES == 2 * HDIM
        and CLUS_DEV * n_seq <= 16
        and projection.shape[2] // n_head == 4 * LANES
        and hidden.shape[2] % (n_head * COLUMNS) == 0
        and tokens % (LANES // 2) == 0
        and tokens <= 2 * LANES
    )


def solution(mesh):
    in_specs = (
        P("dp", "seq", None),
        P(),
        P(None, None, "head"),
        P("dp", "seq", "head"),
        P("dp", "seq", None),
    )
    out_specs = (P("dp", "seq", "head"), P("head"))

    def program(hidden, norm_gain, projection, upstream, cluster):
        body = on_device_heads if splits_by_heads(mesh, hidden, projection) else on_device
        return jax.shard_map(
            body, mesh=mesh, in_specs=in_specs, out_specs=out_specs, check_vma=False
        )(hidden, norm_gain, projection, upstream, cluster)

    return program
```
